32 devices in a mesh: dp: 8 (over z, core), clus: 4 (over y, x).
Axes of the slice: x: 2, y: 2, z: 4, core: 2. Of those that a mesh axis runs over, the one named last changes fastest.
Arguments:
- rows: bfloat16 [8192, 1024], P(('dp', 'clus')), may hold values from -8 to 8
- fine_assign: int32 [8192], P(('dp', 'clus')), may hold values from 0 to 8191, as said below
- parent1: int32 [8192], P(('dp', 'clus')), may hold values from 0 to 2047, as said below
- parent2: int32 [2048], P('dp'), may hold values from 0 to 511
- parent3: int32 [512], replicated, may hold values from 0 to 63
- shrink: float32 [4], replicated, may hold values from 0.5 to 2
Outputs:
- fine_centroids: bfloat16 [8192, 1024], P(('dp', 'clus'))
- mid_centroids: bfloat16 [2048, 1024], P(('dp', 'clus'))
- coarse_centroids: bfloat16 [512, 1024], P(('dp', 'clus'))
- spread: float32 [8192], P(('dp', 'clus'))
The draws below stay inside these ranges and needn't reach their ends.
Inputs may be any that keep to these rules, and one draw needn't show every extreme that they name: `fine_assign`: devices are numbered d = dp index * 4 + clus index, and fine centroid k is owned by device k // 256. Every row of device d names a fine centroid owned by a device of the same dp index. At most 128 rows of one device name centroids of one owner, and in every dp group some owner is named by exactly 128 rows of each device of the group. parent1[k] is one of the 256 second-level centroids g * 256 to g * 256 + 255, with g = k // 1024.
All inputs are finite; a program needn't handle non-finite values.
Results may differ from the reference program's by a relative error of at most 0.0035.
Values may be sent and summed in bfloat16 or wider, within the bound.
A program may use at most 64 MiB of HBM per device.

```python
import math
import jax
import jax.numpy as jnp

D = 1024
ROWS_DEV = 256
F1 = 256
F2 = 256
K3 = 512
K4 = 64
ROWS = 8192
K1 = 8192
K2 = 2048
N_DP = 8
N_CLUS = 4
DEVICES = 32


def make_parent1(key):
    index = jnp.arange(F1 * DEVICES, dtype=jnp.int32)
    group = index // (F1 * N_CLUS)
    pick = jax.random.randint(jax.random.fold_in(key, 11), (F1 * DEVICES,), 0, F2)
    return (group * F2 + pick).astype(jnp.int32)


def make_parent2(key):
    return jax.random.randint(jax.random.fold_in(key, 12), (F2 * N_DP,), 0, K3).astype(jnp.int32)


def make_parent3(key):
    return jax.random.randint(jax.random.fold_in(key, 13), (K3,), 0, K4).astype(jnp.int32)


def make_assign(key):
    base = jax.random.fold_in(key, 14)
    key_full, key_position, key_order, key_local = jax.random.split(base, 4)
    capacity_limit = 2 * ROWS_DEV // N_CLUS
    position_count = N_CLUS * capacity_limit
    full_row = jax.random.randint(key_full, (N_DP,), 0, N_CLUS)
    complete_per_shard = jnp.repeat(full_row, N_CLUS)
    position_index = jnp.arange(position_count, dtype=jnp.int32)
    random_jitter = jax.random.randint(key_position, (DEVICES, position_count), 0, 2 ** 14)
    extra_reward = jnp.where(position_index[None, :] // capacity_limit == complete_per_shard[:, None], 2 ** 28, 0)
    rating_value = random_jitter * position_count + position_index[None, :] + extra_reward
    chosen = jnp.argsort(-rating_value, axis=1)[:, :ROWS_DEV]
    target = (chosen // capacity_limit).astype(jnp.int32)
    mixing = jax.random.randint(key_order, (DEVICES, ROWS_DEV), 0, 2 ** 14) * ROWS_DEV + jnp.arange(ROWS_DEV)[None, :]
    order = jnp.argsort(mixing, axis=1)
    target = jnp.take_along_axis(target, order, axis=1)
    local = jax.random.randint(key_local, (DEVICES, ROWS_DEV), 0, F1)
    dev_dp = (jnp.arange(DEVICES, dtype=jnp.int32) // N_CLUS)[:, None]
    fine = (dev_dp * N_CLUS + target) * F1 + local
    return fine.reshape(-1).astype(jnp.int32)


def offsets(key, labels):
    return jax.vmap(lambda label: jax.random.normal(jax.random.fold_in(key, label), (D,), jnp.float32))(labels)


def draw_fine_assign(key, part):
    return make_assign(key)


def draw_parent1(key, part):
    return make_parent1(key)


def draw_parent2(key, part):
    return make_parent2(key)


def draw_parent3(key, part):
    return make_parent3(key)


def draw_rows(key, part):
    first = make_assign(key)
    second = make_parent1(key)[first]
    third = make_parent2(key)[second]
    fourth = make_parent3(key)[third]
    values = offsets(jax.random.fold_in(key, 21), fourth)
    values = values + 0.8 * offsets(jax.random.fold_in(key, 22), third)
    values = values + 0.6 * offsets(jax.random.fold_in(key, 23), second)
    values = values + 0.5 * offsets(jax.random.fold_in(key, 24), first)
    values = values + 0.5 * jax.random.normal(jax.random.fold_in(key, 25), (ROWS_DEV * DEVICES, D), jnp.float32)
    return jnp.clip(values, -8.0, 8.0).astype(jnp.bfloat16)


def setup_inputs(seed: int = 0) -> dict:
    key_of = jax.random.split(jax.random.key(seed), 7)
    rows = draw_rows(jax.random.fold_in(key_of[6], 71), 0)
    fine_assign = draw_fine_assign(jax.random.fold_in(key_of[6], 71), 0)
    parent1 = draw_parent1(jax.random.fold_in(key_of[6], 71), 0)
    parent2 = draw_parent2(jax.random.fold_in(key_of[6], 71), 0)
    parent3 = draw_parent3(jax.random.fold_in(key_of[6], 71), 0)
    shrink = jnp.clip(jnp.exp(jax.random.uniform(key_of[5], (4,), jnp.float32, math.log(0.5), math.log(2.0))), 0.5, 2.0)
    return dict(rows=rows, fine_assign=fine_assign, parent1=parent1, parent2=parent2, parent3=parent3, shrink=shrink)


def shrunk(sums, counts, prior, weight):
    return (sums + weight * prior) / (counts + weight)[:, None]


def reference(rows, fine_assign, parent1, parent2, parent3, shrink):
    ones = jnp.ones(fine_assign.shape, jnp.float32)
    fine_sums = jax.ops.segment_sum(rows.astype(jnp.float32), fine_assign, num_segments=K1)
    fine_counts = jax.ops.segment_sum(ones, fine_assign, num_segments=K1)
    middle_sums = jax.ops.segment_sum(fine_sums, parent1, num_segments=K2)
    middle_counts = jax.ops.segment_sum(fine_counts, parent1, num_segments=K2)
    third_sums = jax.ops.segment_sum(middle_sums, parent2, num_segments=K3)
    third_counts = jax.ops.segment_sum(middle_counts, parent2, num_segments=K3)
    top_sums = jax.ops.segment_sum(third_sums, parent3, num_segments=K4)
    top_counts = jax.ops.segment_sum(third_counts, parent3, num_segments=K4)
    center = jnp.sum(top_sums, axis=0) / ROWS
    top_means = shrunk(top_sums, top_counts, center[None, :], shrink[0] * (ROWS / K4))
    third_means = shrunk(third_sums, third_counts, top_means[parent3], shrink[1] * (ROWS / K3))
    middle_means = shrunk(middle_sums, middle_counts, third_means[parent2], shrink[2] * (ROWS / K2))
    fine_means = shrunk(fine_sums, fine_counts, middle_means[parent1], shrink[3] * (ROWS / K1))
    fine_out = fine_means.astype(jnp.bfloat16)
    diff = rows.astype(jnp.float32) - fine_out.astype(jnp.float32)[fine_assign]
    error = jnp.sum(diff * diff, axis=1)
    spread = jax.ops.segment_sum(error, fine_assign, num_segments=K1) / (D * (fine_counts + 1.0))
    return fine_out, middle_means.astype(jnp.bfloat16), third_means.astype(jnp.bfloat16), spread
```

```python
import functools

import jax
import jax.numpy as jnp
from jax import lax
from jax.experimental import pallas as pl
from jax.experimental.pallas import tpu as pltpu
from jax.sharding import PartitionSpec as P

K4 = 64


HIGH = lax.Precision.HIGHEST


def shrunk(sums, counts, prior, weight):
    return (sums + weight * prior) / (counts + weight)[:, None]


def local(rows, fine_assign, parent1, parent2, parent3, shrink):
    groups = lax.axis_size("clus")
    dp_count = lax.axis_size("dp")
    devices = groups * dp_count
    clus_index = lax.axis_index("clus")
    dp_index = lax.axis_index("dp")
    count = rows.shape[0]
    width = rows.shape[1]
    fine_dev = parent1.shape[0]
    middle_dp = parent2.shape[0]
    third = parent3.shape[0]
    slots = 2 * count // groups
    total = count * devices
    weight_top = shrink[0] * (total / K4)
    weight_third = shrink[1] * (total / third)
    weight_middle = shrink[2] * (total / (middle_dp * dp_count))
    weight_fine = shrink[3] * (total / (fine_dev * devices))
    local_ids = fine_assign - dp_index * groups * fine_dev
    target = local_ids // fine_dev
    within = local_ids - target * fine_dev
    target_hot = (target[:, None] == jnp.arange(groups)[None, :]).astype(jnp.bfloat16)
    earlier = (jnp.arange(count)[:, None] > jnp.arange(count)[None, :]).astype(jnp.bfloat16)
    before = jnp.dot(earlier, target_hot, preferred_element_type=jnp.float32)
    rank = jnp.sum(before * target_hot.astype(jnp.float32), axis=1).astype(jnp.int32)
    slot_of = target * slots + rank
    source = (
        jnp.full((groups * slots,), count, jnp.int32)
        .at[slot_of]
        .set(jnp.arange(count, dtype=jnp.int32))
    )
    padded = jnp.concatenate([rows, jnp.zeros((1, width), jnp.bfloat16)], axis=0)
    send_rows = padded[source].reshape(groups, slots, width)
    send_ids = jnp.concatenate([within, jnp.full((1,), -1, jnp.int32)])[source].reshape(
        groups, slots
    )
    got_rows, got_ids = (
        lax.all_to_all(send_rows, "clus", split_axis=0, concat_axis=0, tiled=True),
        lax.all_to_all(send_ids, "clus", split_axis=0, concat_axis=0, tiled=True),
    )
    got_rows = got_rows.reshape(groups * slots, width)
    got_ids = got_ids.reshape(groups * slots)
    member = (got_ids[:, None] == jnp.arange(fine_dev)[None, :]).astype(jnp.bfloat16)
    contract = (((0,), (0,)), ((), ()))
    fine_sums = lax.dot_general(member, got_rows, contract, preferred_element_type=jnp.float32)
    fine_counts = jnp.sum(member.astype(jnp.float32), axis=0)
    middle_local = parent1 - dp_index * middle_dp
    child_hot = (jnp.arange(middle_dp)[:, None] == middle_local[None, :]).astype(jnp.float32)
    middle_part = jnp.dot(child_hot, fine_sums, precision=HIGH)
    middle_tally = jnp.dot(child_hot, fine_counts, precision=HIGH)
    share = middle_dp // groups
    offset = clus_index * share
    middle_sums, middle_counts = (
        lax.psum_scatter(middle_part, "clus", scatter_dimension=0, tiled=True),
        lax.psum_scatter(middle_tally, "clus", scatter_dimension=0, tiled=True),
    )
    own_parent2 = lax.dynamic_slice_in_dim(parent2, offset, share, 0)
    third_share = third // devices
    third_start = (dp_index * groups + clus_index) * third_share
    third_hot = (jnp.arange(third)[:, None] == own_parent2[None, :]).astype(jnp.float32)
    third_part = jnp.dot(third_hot, middle_sums, precision=HIGH)
    third_tally = jnp.dot(third_hot, middle_counts, precision=HIGH)
    third_sums, third_counts = lax.psum((third_part, third_tally), ("dp", "clus"))
    top_hot = (jnp.arange(K4)[:, None] == parent3[None, :]).astype(jnp.float32)
    top_sums = jnp.dot(top_hot, third_sums, precision=HIGH)
    top_counts = jnp.dot(top_hot, third_counts, precision=HIGH)
    center = jnp.sum(top_sums, axis=0) / total
    top_means = shrunk(top_sums, top_counts, center[None, :], weight_top)
    third_means = shrunk(
        third_sums, third_counts, jnp.dot(top_hot.T, top_means, precision=HIGH), weight_third
    )
    third_out = lax.dynamic_slice_in_dim(third_means, third_start, third_share, 0)
    parent_hot = (own_parent2[:, None] == jnp.arange(third)[None, :]).astype(jnp.float32)
    middle_out = shrunk(
        middle_sums, middle_counts, jnp.dot(parent_hot, third_means, precision=HIGH), weight_middle
    )
    middle_means = lax.all_gather(middle_out, "clus", axis=0, tiled=True)
    fine_means = shrunk(
        fine_sums, fine_counts, jnp.dot(child_hot.T, middle_means, precision=HIGH), weight_fine
    )
    fine_out = fine_means.astype(jnp.bfloat16)
    back = jnp.dot(member, fine_out, preferred_element_type=jnp.float32)
    diff = got_rows.astype(jnp.float32) - back
    row_error = jnp.sum(diff * diff, axis=1)
    spread = jnp.sum(member.astype(jnp.float32) * row_error[:, None], axis=0) / (
        width * (fine_counts + 1.0)
    )
    return (fine_out, middle_out.astype(jnp.bfloat16), third_out.astype(jnp.bfloat16), spread)


LANES = 128
HALF = LANES // 2
BF = jnp.bfloat16
F32 = jnp.float32
MESH = pl.DeviceIdType.MESH


def rows_hot(size, ids):
    shape = (size, ids.shape[1])
    return jnp.where(lax.broadcasted_iota(jnp.int32, shape, 0) == ids, 1.0, 0.0).astype(BF)


def column_of(ids):
    return jnp.broadcast_to(ids.astype(F32), (LANES, ids.shape[1])).T


def lanes_hot(column, start):
    lane = lax.broadcasted_iota(jnp.int32, column.shape, 1).astype(F32) + float(start)
    return jnp.where(column == lane, 1.0, 0.0).astype(BF)


def dot(a, b):
    return jnp.dot(a, b, preferred_element_type=F32)


def pieces(x, count):
    out = []
    for _ in range(count):
        part = x.astype(BF)
        out.append(part)
        x = x - part.astype(F32)
    return out


def dot_left(x, hot, count=3):
    return sum(dot(part, hot) for part in pieces(x, count))


def halves(a, b, part):
    lane = slice(part * HALF, (part + 1) * HALF)
    return jnp.concatenate([a[:, lane], b[:, lane]], axis=1)


def dot_stack(x, hot):
    both = dot(jnp.concatenate(pieces(x, 2), axis=0), hot)
    return both[: x.shape[0]] + both[x.shape[0] :]


def sweep(
    n,
    m,
    fa_hbm,
    p1_hbm,
    p2_hbm,
    p3_hbm,
    shrink_hbm,
    rows_ref,
    fine_ref,
    mid_ref,
    coarse_ref,
    spread_ref,
    fa_all,
    p1_all,
    p2_all,
    p3_ref,
    shrink_ref,
    rows_own,
    row_out,
    row_in,
    got,
    h1f,
    h2f,
    h1r,
    h1m,
    ht,
    hn,
    sums2,
    base1,
    pull1,
    scale2,
    rate1,
    part_own,
    part_all,
    cnt_own,
    cnt_all,
    cnt_third,
    cnt_top,
    means3,
    back_own,
    back_all,
    coarse_all,
    mid_half,
    fine_out,
    fine_in,
    fine_own,
    mid_own,
    coarse_own,
    err_own,
    err_all,
    tally,
    in_sem,
    id_send,
    id_recv,
    p2_send,
    p2_recv,
    row_send,
    row_recv,
    part_send,
    part_recv,
    cnt_send,
    cnt_recv,
    back_send,
    back_recv,
    fine_send,
    fine_recv,
    mid_send,
    mid_recv,
    out_send,
    out_recv,
    err_send,
    err_recv,
    local_sem,
):
    me = lax.axis_index("clus")
    dp = lax.axis_index("dp")
    count, width = rows_ref.shape
    share = width // n
    tiles = share // LANES
    chunks = 2 * tiles
    fine_dev = p1_hbm.shape[1]
    middle = p2_hbm.shape[1]
    third = p3_hbm.shape[1]
    devices = n * m
    total = count * devices
    fine = n * fine_dev
    some = count // 2
    few = fine_dev // 2
    packed = n * some
    center_dp = m // 2 // 2 * 2
    pairs = m // 2
    pair = dp // 2
    side = lax.rem(dp, 2)
    near = (center_dp // 2 - 1, center_dp // 2)
    far = (0, pairs - 1)
    plan = [far if q == 2 else near for q in range(chunks)]
    size = 4
    thin = HALF // size
    window = third // pairs
    mid_share = middle // n
    third_share = third // devices

    def span(index, size):
        return pl.ds(pl.multiple_of(index * size, size), size)

    def tile_of(t):
        return slice(t * LANES, (t + 1) * LANES)

    def column(index, t):
        return pl.ds(pl.multiple_of(index * share + t * LANES, LANES), LANES)

    def remote(src, dst, send, recv, device):
        return pltpu.make_async_remote_copy(
            src_ref=src,
            dst_ref=dst,
            send_sem=send,
            recv_sem=recv,
            device_id=device,
            device_id_type=MESH,
        )

    if n == 4:
        peers = [n - 1 - me, lax.rem(me + 2, n), me + 1 - 2 * lax.rem(me, 2)]
    else:
        peers = [lax.rem(me + k, n) for k in range(1, n)]

    def dp_peer(k):
        return lax.rem(dp + k, m)

    started = []

    def start(copies):
        for copy in copies:
            copy.start()
        started.extend(copies)
        return copies

    def arrive(copies):
        for copy in copies:
            copy.wait_recv()

    low_half = pair < pairs // 2

    def close(q):
        return jnp.where(low_half, plan[q][0], plan[q][1])

    def owners(q):
        other = jnp.where(low_half, plan[q][1], plan[q][0])
        block = jnp.where(low_half, 2, 0)
        own = 2 - block
        return (
            (other * 2, block),
            (other * 2 + 1, block + 1),
            (close(q) * 2 + 1 - side, own + 1 - side),
            (close(q) * 2 + side, own + side),
        )

    def is_owner(q):
        return pair == close(q)

    def slot(q):
        return owners(q)[3][1]

    if pairs == 4:
        inward = jnp.where(low_half, pair + 1, pair - 1)
        last = jnp.where(low_half, 3, 0)
        chips = [inward, 6 - pair - inward - last, last]
    else:
        chips = [lax.rem(pair + k, pairs) for k in range(1, pairs)]
    others = [chip * 2 + core for chip in reversed(chips) for core in range(2)]
    others.append(pair * 2 + 1 - side)

    barrier = pltpu.get_barrier_semaphore()
    for peer in peers:
        pl.semaphore_signal(barrier, inc=1, device_id={"clus": peer}, device_id_type=MESH)
    for k in range(1, m):
        pl.semaphore_signal(barrier, inc=1, device_id={"dp": dp_peer(k)}, device_id_type=MESH)
    fetch = [
        pltpu.make_async_copy(src, dst, in_sem.at[i])
        for i, (src, dst) in enumerate(
            [
                (fa_hbm, fa_all.at[me]),
                (p1_hbm, p1_all.at[me]),
                (p2_hbm, p2_all.at[dp]),
                (rows_ref, rows_own),
                (p3_hbm, p3_ref),
                (shrink_hbm, shrink_ref),
            ]
        )
    ]
    for copy in fetch:
        copy.start()
    pl.semaphore_wait(barrier, n - 1 + m - 1)
    for copy in fetch[:3]:
        copy.wait()

    id_copies = []
    for k, peer in enumerate(peers):
        for which, ids in enumerate((fa_all, p1_all)):
            own = ids.at[me]
            id_copies.append(
                remote(own, own, id_send.at[which, k], id_recv.at[which, k], {"clus": peer})
            )
    start(id_copies)
    start(
        [
            remote(
                p2_all.at[dp], p2_all.at[dp], p2_send.at[k], p2_recv.at[dp], {"dp": dp_peer(k)}
            )
            for k in range(1, m)
        ]
    )
    fetch[3].wait()
    row_copies = []
    for q in range(chunks):
        t, a = divmod(q, 2)
        for p in range(n):
            lane = slice(p * share + t * LANES, p * share + (t + 1) * LANES)
            row_out[q, p] = halves(rows_own[0:some, lane], rows_own[some:count, lane], a)
        row_copies.append(
            start(
                [
                    remote(
                        row_out.at[q, peer],
                        row_in.at[q, span(me, some), :],
                        row_send.at[q, k],
                        row_recv.at[q, k],
                        {"clus": peer},
                    )
                    for k, peer in enumerate(peers)
                ]
            )
        )
        row_in[q, span(me, some), :] = row_out[q, me]

    for copy in fetch[4:]:
        copy.wait()
    w4 = shrink_ref[0] * (total / K4)
    w3 = shrink_ref[1] * (total / third)
    w2 = shrink_ref[2] * (total / (middle * m))
    w1 = shrink_ref[3] * (total / (fine_dev * devices))
    p3_row = p3_ref[...]
    h4 = lanes_hot(column_of(p3_row), 0)
    h4f = rows_hot(LANES, p3_row)
    ones = jnp.ones((LANES, LANES), BF)

    def left_half(size):
        return lax.broadcasted_iota(jnp.int32, (size, LANES), 1) < HALF

    def parents_of(i, own):
        if not own:
            block = p2_all.at[i]
            remote(block, block, p2_send.at[0], p2_recv.at[i], {"dp": i}).wait_recv()
        row = p2_all[i]
        ht[:, span(i, middle)] = rows_hot(third, row)
        p2_column = column_of(row)
        for j in range(0, third, LANES):
            hn[span(i, middle), j : j + LANES] = lanes_hot(p2_column, j)

    parents_of(dp, True)
    parents_of(pair * 2 + 1 - side, False)
    parents_of(chips[0] * 2, False)
    parents_of(chips[0] * 2 + 1, False)
    arrive(id_copies)
    ids = [fa_all[i] for i in range(n)]
    ids = [x[:, 0:some] for x in ids] + [x[:, some:count] for x in ids]
    fa_row = jnp.concatenate(ids, axis=1) - dp * fine
    table = [
        p1_all[i][:, j : j + LANES] for i in range(n) for j in range(0, fine_dev, LANES)
    ]
    table = (jnp.concatenate(table, axis=0) - dp * middle).astype(F32).astype(BF)
    line = fa_row // LANES
    picked = dot(table, rows_hot(LANES, fa_row - line * LANES))
    lines = lax.broadcasted_iota(jnp.int32, picked.shape, 0)
    mid_row = jnp.sum(jnp.where(lines == line, picked, 0.0), axis=0, keepdims=True)
    h2f[...] = rows_hot(middle, mid_row.astype(jnp.int32))

    def part_copy(q, k):
        device, o = owners(q)[k]
        return remote(
            part_own.at[q, span(o, thin), :],
            part_all.at[q, dp],
            part_send.at[q, k],
            part_recv.at[q, dp],
            {"dp": device},
        )

    def part_from(q, i):
        block = part_all.at[q, i]
        return remote(block, block, part_send.at[q, 0], part_recv.at[q, i], {"dp": i})

    def cnt_copy(k):
        peer = dp_peer(k)
        return remote(cnt_own, cnt_all.at[dp], cnt_send.at[k], cnt_recv.at[dp], {"dp": peer})

    def cnt_from(i):
        return remote(cnt_own, cnt_all.at[i], cnt_send.at[0], cnt_recv.at[i], {"dp": i})

    def sum_part(q):
        arrive(row_copies[q])
        block = row_in[q]
        both = jnp.where(
            left_half(middle), dot(h2f[:, 0:packed], block), dot(h2f[:, packed:], block)
        )
        both = both + pltpu.roll(both, HALF, 1)
        part_own[q] = both.T[0:HALF].astype(BF)
        for k in range(size - 1):
            part_copy(q, k).start()

        @pl.when(is_owner(q))
        def _():
            part_all[q, dp] = part_own[q, span(slot(q), thin), :]

        @pl.when(jnp.logical_not(is_owner(q)))
        def _():
            part_copy(q, size - 1).start()

        sums2[q] = both

    count2 = h2f[:, 0:LANES]
    for j in range(LANES, n * count, LANES):
        count2 = count2 + h2f[:, j : j + LANES]
    count2 = dot(count2, ones)
    cnt_own[...] = count2.T[0:1]
    for k in range(1, m):
        cnt_copy(k).start()
    cnt_all[dp] = cnt_own[...]
    sum_part(0)
    for chip in chips[1:]:
        parents_of(chip * 2, False)
        parents_of(chip * 2 + 1, False)

    def back_copy(q, k):
        peer = others[k]
        return remote(
            back_own.at[q, :, span(peer, middle)],
            back_all.at[q, span(slot(q), thin), :],
            back_send.at[0, q, k],
            back_recv.at[0, q, slot(q)],
            {"dp": peer},
        )

    def coarse_copy(q, k):
        peer = others[k]
        return remote(
            means3.at[q, :, span(peer // 2, window)],
            coarse_all.at[q, span(slot(q), thin), :],
            back_send.at[1, q, k],
            back_recv.at[1, q, slot(q)],
            {"dp": peer},
        )

    def from_owners(which, q):
        dst = (back_all, coarse_all)[which]

        def wait(k):
            device, o = owners(q)[k]
            block = dst.at[q, span(o, thin), :]
            send, recv = back_send.at[which, q, 0], back_recv.at[which, q, o]
            remote(block, block, send, recv, {"dp": device}).wait_recv()

        for k in range(size - 1):
            wait(k)

        @pl.when(jnp.logical_not(is_owner(q)))
        def _():
            wait(size - 1)

    def third_level(q):
        total3 = jnp.zeros((thin + 16, third), F32)
        if q == plan.index(plan[q]):
            for i in others:
                cnt_from(i).wait_recv()
        for chip in (pair, *chips):
            for i in (chip * 2, chip * 2 + 1) if chip is not pair else (pair * 2 + 1 - side,):
                part_from(q, i).wait_recv()
            block = jnp.concatenate([part_all[q, chip * 2 + c] for c in range(2)], axis=1)
            if q == plan.index(plan[q]):
                lines = jnp.concatenate([cnt_all[chip * 2 + c] for c in range(2)], axis=1)
                row = lax.broadcasted_iota(jnp.int32, (16, 2 * middle), 0)
                stack = jnp.zeros((16, 2 * middle), F32)
                for i, part in enumerate(pieces(lines, 3)):
                    stack = jnp.where(row == i, part.astype(F32), stack)
                block = jnp.concatenate([block, stack.astype(BF)], axis=0)
                total3 = total3 + dot(block, hn[span(chip, 2 * middle), :])
            else:
                total3 = total3[0:thin] + dot(block, hn[span(chip, 2 * middle), :])
        sums3 = total3[0:thin]
        if q == plan.index(plan[q]):
            cnt3 = total3[thin : thin + 1] + total3[thin + 1 : thin + 2] + total3[thin + 2 : thin + 3]
            cnt_third[...] = cnt3
            both = jnp.concatenate([sums3, jnp.broadcast_to(cnt3, (16, third))], axis=0)
            both = dot_stack(both, h4)
            sums4, cnt4 = both[0:thin], both[thin : thin + 1]
            cnt_top[...] = cnt4
        else:
            cnt3, cnt4 = cnt_third[...], cnt_top[...]
            sums4 = dot_stack(sums3, h4)
        center = jnp.sum(sums4, axis=1, keepdims=True) / total
        means4 = (sums4 + w4 * center) / (cnt4 + w4)
        block = ((sums3 + w3 * dot_stack(means4, h4f)) / (cnt3 + w3)).astype(BF)
        means3[q] = block
        back_own[q] = dot(block, ht[...]).astype(BF)
        for k in range(m - 1):
            back_copy(q, k).start()
        for k in range(m - 1):
            coarse_copy(q, k).start()
        back_all[q, span(slot(q), thin), :] = back_own[q, :, span(dp, middle)]
        coarse_all[q, span(slot(q), thin), :] = means3[q, :, span(dp // 2, window)]

    def run_third(q):
        @pl.when(is_owner(q))
        def _():
            third_level(q)

    def unpack(t):
        a, b = row_in[2 * t], row_in[2 * t + 1]
        got[0:packed, tile_of(t)] = halves(a, b, 0)
        got[packed:, tile_of(t)] = halves(a, b, 1)

    def fine_counts():
        some_counts = h1f[:, 0:LANES]
        for j in range(LANES, n * count, LANES):
            some_counts = some_counts + h1f[:, j : j + LANES]
        return dot(some_counts, ones)

    def bases(t):
        unpack(t)
        left = left_half(few)
        if t == 0:
            scale2[...] = 1.0 / (count2 + w2)
            rate1[...] = 1.0 / (fine_counts() + w1)
        sums1 = dot(h1f[...], got[:, tile_of(t)])
        for p in range(n):
            low = slice(p * fine_dev, p * fine_dev + few)
            high = slice(p * fine_dev + few, (p + 1) * fine_dev)
            place = slice(p * few, (p + 1) * few)
            rate_a, rate_b = rate1[low], rate1[high]
            if t == 0:
                pull1[place, :] = w1 * jnp.where(left, rate_a, rate_b)
            a = sums1[low] * rate_a
            b = sums1[high] * rate_b
            base1[2 * t, place, :] = halves(a, b, 0)
            base1[2 * t + 1, place, :] = halves(a, b, 1)

    fine_copies = []
    mid_copies = []
    local_copies = []

    def down(q):
        t, a = divmod(q, 2)
        from_owners(0, q)
        prior2 = back_all[q].astype(F32)
        prior2 = jnp.concatenate([prior2, prior2], axis=0).T
        means2 = (sums2[q] + w2 * prior2) * scale2[...]
        prior1 = sum(dot(h1m[...], part) for part in pieces(means2, 2))
        left = left_half(few)
        for p in range(n):
            low = prior1[p * fine_dev : p * fine_dev + few]
            high = prior1[p * fine_dev + few : (p + 1) * fine_dev]
            place = slice(p * few, (p + 1) * few)
            means1 = base1[q, place] + pull1[place] * jnp.where(left, low, high)
            fine_out[q, p] = means1.astype(BF)
        copies = start(
            [
                remote(
                    fine_out.at[q, peer],
                    fine_in.at[q, me],
                    fine_send.at[q, k],
                    fine_recv.at[q, k],
                    {"clus": peer},
                )
                for k, peer in enumerate(peers)
            ]
        )
        fine_copies.append(copies)
        if not a:
            mid_half[...] = means2
            return
        mid_own[:, tile_of(t)] = jnp.where(left_half(middle), mid_half[...], means2).astype(BF)
        for k, peer in enumerate(peers):
            mid_copies.extend(
                start(
                    [
                        remote(
                            mid_own.at[span(peer, mid_share), tile_of(t)],
                            mid_ref.at[:, column(me, t)],
                            mid_send.at[t, k],
                            mid_recv.at[t, k],
                            {"clus": peer},
                        )
                    ]
                )
            )
        copy = pltpu.make_async_copy(
            mid_own.at[span(me, mid_share), tile_of(t)], mid_ref.at[:, column(me, t)], local_sem.at[t]
        )
        copy.start()
        local_copies.append(copy)

    def rows_by_fine():
        fa_column = column_of(fa_row)
        for j in range(0, fine, LANES):
            h1r[:, j : j + LANES] = lanes_hot(fa_column, j)

    def coarse(t):
        for q in (2 * t, 2 * t + 1):
            from_owners(1, q)
        block = jnp.concatenate([coarse_all[2 * t], coarse_all[2 * t + 1]], axis=0)
        coarse_own[:, tile_of(t)] = block.astype(F32).T.astype(BF)

        def place(peer):
            return coarse_own.at[span(side * n + peer, third_share), tile_of(t)]

        out_copies.extend(
            start(
                [
                    remote(
                        place(peer),
                        coarse_ref.at[:, column(me, t)],
                        out_send.at[t, k],
                        out_recv.at[t, k],
                        {"clus": peer},
                    )
                    for k, peer in enumerate(peers)
                ]
            )
        )
        copy = pltpu.make_async_copy(
            place(me), coarse_ref.at[:, column(me, t)], local_sem.at[tiles + t]
        )
        copy.start()
        local_copies.append(copy)

    def fine_tile(t):
        for p in range(n):
            a, b = fine_out[2 * t, p], fine_out[2 * t + 1, p]
            fine_own[p * fine_dev : p * fine_dev + few, tile_of(t)] = halves(a, b, 0)
            fine_own[p * fine_dev + few : (p + 1) * fine_dev, tile_of(t)] = halves(a, b, 1)

    out_copies = []
    p1_row = jnp.concatenate([p1_all[i] for i in range(n)], axis=1) - dp * middle
    p1_column = column_of(p1_row)
    for j in range(0, middle, LANES):
        h1m[:, j : j + LANES] = lanes_hot(p1_column, j)
    sum_part(1)
    h1f[...] = rows_hot(fine, fa_row)
    for q in range(2, chunks - 1):
        sum_part(q)
    bases(0)
    run_third(0)
    sum_part(chunks - 1)
    run_third(1)
    for t in range(1, tiles):
        bases(t)
    run_third(2)
    down(0)
    for q in range(3, chunks):
        run_third(q)
    for q in range(1, chunks):
        down(q)
        if q % 2 and q < chunks - 1:
            coarse(q // 2)
            fine_tile(q // 2)
            rows_by_fine()
    if chunks == 2:
        rows_by_fine()
    coarse(tiles - 1)
    fine_tile(tiles - 1)
    fine_ref[:, span(me, share)] = fine_own[span(me, fine_dev), :]
    diff = got[...].astype(F32) - dot(h1r[...], fine_own[...])
    square = diff * diff
    folded = square[:, :LANES]
    for j in range(LANES, share, LANES):
        folded = folded + square[:, j : j + LANES]
    square = folded
    err_row = jnp.sum(square.T, axis=0, keepdims=True)
    parts = pieces(err_row, 3)
    line = lax.broadcasted_iota(jnp.int32, (16, n * count), 0)
    stack = jnp.where(line == 3, 1.0, 0.0)
    for i, part in enumerate(parts):
        stack = jnp.where(line == i, part.astype(F32), stack)
    by_fine = dot(stack.astype(BF), h1r[...])
    err_fine = by_fine[0:1] + by_fine[1:2] + by_fine[2:3]
    for i in range(n):
        err_own[i] = err_fine[:, i * fine_dev : (i + 1) * fine_dev]
        tally[i] = by_fine[3:4, i * fine_dev : (i + 1) * fine_dev]
    err_copies = start(
        [
            remote(
                err_own.at[peer],
                err_all.at[me],
                err_send.at[k],
                err_recv.at[k],
                {"clus": peer},
            )
            for k, peer in enumerate(peers)
        ]
    )
    err_all[me] = err_own[me]

    for t in range(tiles):
        for q in (2 * t, 2 * t + 1):
            arrive(fine_copies[q])
        for k in range(1, n):
            peer = lax.rem(me + k, n)
            a, b = fine_in[2 * t, peer], fine_in[2 * t + 1, peer]
            fine_ref[0:few, column(peer, t)] = halves(a, b, 0)
            fine_ref[few:, column(peer, t)] = halves(a, b, 1)
    arrive(err_copies)
    err = err_all[0]
    for i in range(1, n):
        err = err + err_all[i]
    spread_ref[...] = err / (width * (tally[me] + 1.0))
    for copy in local_copies:
        copy.wait()
    arrive(mid_copies)
    arrive(out_copies)
    for copy in started:
        copy.wait_send()
    for k in range(1, m):
        cnt_copy(k).wait_send()
    for q in range(chunks):
        for k in range(size - 1):
            part_copy(q, k).wait_send()

    def drain(q):
        @pl.when(is_owner(q))
        def _():
            for k in range(m - 1):
                back_copy(q, k).wait_send()
                coarse_copy(q, k).wait_send()

        @pl.when(jnp.logical_not(is_owner(q)))
        def _():
            part_copy(q, size - 1).wait_send()

    for q in range(chunks):
        drain(q)


def land(count, *refs):
    sem = refs[-1]
    pairs = zip(refs[:count], refs[count : 2 * count])
    copies = [pltpu.make_async_copy(a, b, sem.at[i]) for i, (a, b) in enumerate(pairs)]
    for copy in copies:
        copy.start()
    for copy in copies:
        copy.wait()


def settle(*arrays):
    count = len(arrays)
    return pl.pallas_call(
        functools.partial(land, count),
        out_shape=tuple(jax.ShapeDtypeStruct(a.shape, a.dtype) for a in arrays),
        in_specs=[pl.BlockSpec(memory_space=pltpu.VMEM)] * count,
        out_specs=tuple([pl.BlockSpec(memory_space=pl.ANY)] * count),
        scratch_shapes=[pltpu.SemaphoreType.DMA((count,))],
        compiler_params=pltpu.CompilerParams(vmem_limit_bytes=4 << 20),
        name="settle",
    )(*arrays)


def fused(rows, fine_assign, parent1, parent2, parent3, shrink):
    n = lax.axis_size("clus")
    m = lax.axis_size("dp")
    count, width = rows.shape
    fine_dev = parent1.shape[0]
    middle = parent2.shape[0]
    third = parent3.shape[0]
    share = width // n
    tiles = share // LANES
    chunks = 2 * tiles
    window = third // (m // 2)
    fine = n * fine_dev
    total_rows = n * count
    vmem = pl.BlockSpec(memory_space=pltpu.VMEM)
    hbm = pl.BlockSpec(memory_space=pltpu.HBM)
    dma = pltpu.SemaphoreType.DMA

    def stay(x):
        return pltpu.with_memory_space_constraint(x, pltpu.HBM)

    fine_out, mid_out, coarse_out, spread = pl.pallas_call(
        functools.partial(sweep, n, m),
        out_shape=(
            jax.ShapeDtypeStruct((fine_dev, width), BF),
            jax.ShapeDtypeStruct((middle // n, width), BF),
            jax.ShapeDtypeStruct((third // (n * m), width), BF),
            jax.ShapeDtypeStruct((1, fine_dev), F32),
        ),
        in_specs=[hbm] * 6,
        out_specs=[vmem] * 4,
        scratch_shapes=[
            pltpu.VMEM((n, 1, count), jnp.int32),
            pltpu.VMEM((n, 1, fine_dev), jnp.int32),
            pltpu.VMEM((m, 1, middle), jnp.int32),
            pltpu.VMEM((1, third), jnp.int32),
            pltpu.SMEM((4,), F32),
            pltpu.VMEM((count, width), BF),
            pltpu.VMEM((chunks, n, count // 2, LANES), BF),
            pltpu.VMEM((chunks, total_rows // 2, LANES), BF),
            pltpu.VMEM((total_rows, share), BF),
            pltpu.VMEM((fine, total_rows), BF),
            pltpu.VMEM((middle, total_rows), BF),
            pltpu.VMEM((total_rows, fine), BF),
            pltpu.VMEM((fine, middle), BF),
            pltpu.VMEM((third, m * middle), BF),
            pltpu.VMEM((m * middle, third), BF),
            pltpu.VMEM((chunks, middle, LANES), F32),
            pltpu.VMEM((chunks, fine // 2, LANES), F32),
            pltpu.VMEM((fine // 2, LANES), F32),
            pltpu.VMEM((middle, LANES), F32),
            pltpu.VMEM((fine, LANES), F32),
            pltpu.VMEM((chunks, HALF, middle), BF),
            pltpu.VMEM((chunks, m, HALF // 4, middle), BF),
            pltpu.VMEM((1, middle), F32),
            pltpu.VMEM((m, 1, middle), F32),
            pltpu.VMEM((1, third), F32),
            pltpu.VMEM((1, LANES), F32),
            pltpu.VMEM((chunks, HALF // 4, third), BF),
            pltpu.VMEM((chunks, HALF // 4, m * middle), BF),
            pltpu.VMEM((chunks, HALF, middle), BF),
            pltpu.VMEM((chunks, HALF, window), BF),
            pltpu.VMEM((middle, LANES), F32),
            pltpu.VMEM((chunks, n, fine_dev // 2, LANES), BF),
            pltpu.VMEM((chunks, n, fine_dev // 2, LANES), BF),
            pltpu.VMEM((fine, share), BF),
            pltpu.VMEM((middle, share), BF),
            pltpu.VMEM((window, share), BF),
            pltpu.VMEM((n, 1, fine_dev), F32),
            pltpu.VMEM((n, 1, fine_dev), F32),
            pltpu.VMEM((n, 1, fine_dev), F32),
            dma((6,)),
            dma((2, n)),
            dma((2, n)),
            dma((m,)),
            dma((m,)),
            dma((chunks, n)),
            dma((chunks, n)),
            dma((chunks, 4)),
            dma((chunks, m)),
            dma((m,)),
            dma((m,)),
            dma((2, chunks, m)),
            dma((2, chunks, 4)),
            dma((chunks, n)),
            dma((chunks, n)),
            dma((tiles, n)),
            dma((tiles, n)),
            dma((tiles, n)),
            dma((tiles, n)),
            dma((n,)),
            dma((n,)),
            dma((2 * tiles,)),
        ],
        compiler_params=pltpu.CompilerParams(
            collective_id=0, has_side_effects=True, vmem_limit_bytes=40 << 20
        ),
        name="sweep",
    )(
        stay(fine_assign.reshape(1, count)),
        stay(parent1.reshape(1, fine_dev)),
        stay(parent2.reshape(1, middle)),
        stay(parent3.reshape(1, third)),
        stay(shrink),
        stay(rows),
    )
    fine_out, mid_out, coarse_out, spread = settle(fine_out, mid_out, coarse_out, spread)
    return fine_out, mid_out, coarse_out, spread.reshape(fine_dev)


def fits(rows, fine_assign, parent1, parent2, parent3):
    n = lax.axis_size("clus")
    m = lax.axis_size("dp")
    return (
        rows.shape[1] % (n * LANES) == 0
        and m % 2 == 0
        and m >= 4
        and rows.shape[0] % (2 * LANES) == 0
        and parent1.shape[0] % LANES == 0
        and parent2.shape[0] % LANES == 0
        and parent2.shape[0] <= 256
        and parent2.shape[0] % (n * 16) == 0
        and parent3.shape[0] % (m // 2 * LANES) == 0
        and parent3.shape[0] % (n * m * 16) == 0
    )


def step(rows, fine_assign, parent1, parent2, parent3, shrink):
    form = fused if fits(rows, fine_assign, parent1, parent2, parent3) else local
    return form(rows, fine_assign, parent1, parent2, parent3, shrink)


def solution(mesh):
    placed = (P(("dp", "clus"), None), P(("dp", "clus")), P(("dp", "clus")), P("dp"), P(), P())
    return jax.shard_map(
        step,
        mesh=mesh,
        in_specs=placed,
        out_specs=(
            P(("dp", "clus"), None),
            P(("dp", "clus"), None),
            P(("dp", "clus"), None),
            P(("dp", "clus")),
        ),
        check_vma=False,
    )
```

```python
import functools

import jax
import jax.numpy as jnp
from jax import lax
from jax.experimental import pallas as pl
from jax.experimental.pallas import tpu as pltpu
from jax.sharding import PartitionSpec as P

K4 = 64


HIGH = lax.Precision.HIGHEST


def shrunk(sums, counts, prior, weight):
    return (sums + weight * prior) / (counts + weight)[:, None]


def local(rows, fine_assign, parent1, parent2, parent3, shrink):
    groups = lax.axis_size("clus")
    dp_count = lax.axis_size("dp")
    devices = groups * dp_count
    clus_index = lax.axis_index("clus")
    dp_index = lax.axis_index("dp")
    count = rows.shape[0]
    width = rows.shape[1]
    fine_dev = parent1.shape[0]
    middle_dp = parent2.shape[0]
    third = parent3.shape[0]
    slots = 2 * count // groups
    total = count * devices
    weight_top = shrink[0] * (total / K4)
    weight_third = shrink[1] * (total / third)
    weight_middle = shrink[2] * (total / (middle_dp * dp_count))
    weight_fine = shrink[3] * (total / (fine_dev * devices))
    local_ids = fine_assign - dp_index * groups * fine_dev
    target = local_ids // fine_dev
    within = local_ids - target * fine_dev
    target_hot = (target[:, None] == jnp.arange(groups)[None, :]).astype(jnp.bfloat16)
    earlier = (jnp.arange(count)[:, None] > jnp.arange(count)[None, :]).astype(jnp.bfloat16)
    before = jnp.dot(earlier, target_hot, preferred_element_type=jnp.float32)
    rank = jnp.sum(before * target_hot.astype(jnp.float32), axis=1).astype(jnp.int32)
    slot_of = target * slots + rank
    source = (
        jnp.full((groups * slots,), count, jnp.int32)
        .at[slot_of]
        .set(jnp.arange(count, dtype=jnp.int32))
    )
    padded = jnp.concatenate([rows, jnp.zeros((1, width), jnp.bfloat16)], axis=0)
    send_rows = padded[source].reshape(groups, slots, width)
    send_ids = jnp.concatenate([within, jnp.full((1,), -1, jnp.int32)])[source].reshape(
        groups, slots
    )
    got_rows, got_ids = (
        lax.all_to_all(send_rows, "clus", split_axis=0, concat_axis=0, tiled=True),
        lax.all_to_all(send_ids, "clus", split_axis=0, concat_axis=0, tiled=True),
    )
    got_rows = got_rows.reshape(groups * slots, width)
    got_ids = got_ids.reshape(groups * slots)
    member = (got_ids[:, None] == jnp.arange(fine_dev)[None, :]).astype(jnp.bfloat16)
    contract = (((0,), (0,)), ((), ()))
    fine_sums = lax.dot_general(member, got_rows, contract, preferred_element_type=jnp.float32)
    fine_counts = jnp.sum(member.astype(jnp.float32), axis=0)
    middle_local = parent1 - dp_index * middle_dp
    child_hot = (jnp.arange(middle_dp)[:, None] == middle_local[None, :]).astype(jnp.float32)
    middle_part = jnp.dot(child_hot, fine_sums, precision=HIGH)
    middle_tally = jnp.dot(child_hot, fine_counts, precision=HIGH)
    share = middle_dp // groups
    offset = clus_index * share
    middle_sums, middle_counts = (
        lax.psum_scatter(middle_part, "clus", scatter_dimension=0, tiled=True),
        lax.psum_scatter(middle_tally, "clus", scatter_dimension=0, tiled=True),
    )
    own_parent2 = lax.dynamic_slice_in_dim(parent2, offset, share, 0)
    third_share = third // devices
    third_start = (dp_index * groups + clus_index) * third_share
    third_hot = (jnp.arange(third)[:, None] == own_parent2[None, :]).astype(jnp.float32)
    third_part = jnp.dot(third_hot, middle_sums, precision=HIGH)
    third_tally = jnp.dot(third_hot, middle_counts, precision=HIGH)
    third_sums, third_counts = lax.psum((third_part, third_tally), ("dp", "clus"))
    top_hot = (jnp.arange(K4)[:, None] == parent3[None, :]).astype(jnp.float32)
    top_sums = jnp.dot(top_hot, third_sums, precision=HIGH)
    top_counts = jnp.dot(top_hot, third_counts, precision=HIGH)
    center = jnp.sum(top_sums, axis=0) / total
    top_means = shrunk(top_sums, top_counts, center[None, :], weight_top)
    third_means = shrunk(
        third_sums, third_counts, jnp.dot(top_hot.T, top_means, precision=HIGH), weight_third
    )
    third_out = lax.dynamic_slice_in_dim(third_means, third_start, third_share, 0)
    parent_hot = (own_parent2[:, None] == jnp.arange(third)[None, :]).astype(jnp.float32)
    middle_out = shrunk(
        middle_sums, middle_counts, jnp.dot(parent_hot, third_means, precision=HIGH), weight_middle
    )
    middle_means = lax.all_gather(middle_out, "clus", axis=0, tiled=True)
    fine_means = shrunk(
        fine_sums, fine_counts, jnp.dot(child_hot.T, middle_means, precision=HIGH), weight_fine
    )
    fine_out = fine_means.astype(jnp.bfloat16)
    back = jnp.dot(member, fine_out, preferred_element_type=jnp.float32)
    diff = got_rows.astype(jnp.float32) - back
    row_error = jnp.sum(diff * diff, axis=1)
    spread = jnp.sum(member.astype(jnp.float32) * row_error[:, None], axis=0) / (
        width * (fine_counts + 1.0)
    )
    return (fine_out, middle_out.astype(jnp.bfloat16), third_out.astype(jnp.bfloat16), spread)


LANES = 128
HALF = LANES // 2
BF = jnp.bfloat16
F32 = jnp.float32
MESH = pl.DeviceIdType.MESH


def rows_hot(size, ids):
    shape = (size, ids.shape[1])
    lines = lax.broadcasted_iota(jnp.int16, shape, 0)
    same = lines == jnp.broadcast_to(ids.astype(jnp.int16), shape)
    return jnp.where(same, jnp.ones(shape, BF), jnp.zeros(shape, BF))


def column_of(ids):
    column = jnp.broadcast_to(ids.astype(F32), (LANES, ids.shape[1])).T
    return column.astype(jnp.int32).astype(jnp.int16)


def lanes_hot(column, start):
    shape = column.shape
    same = column == lax.broadcasted_iota(jnp.int16, shape, 1) + jnp.int16(start)
    return jnp.where(same, jnp.ones(shape, BF), jnp.zeros(shape, BF))


def dot(a, b):
    return jnp.dot(a, b, preferred_element_type=F32)


def pieces(x, count):
    out = []
    for _ in range(count):
        part = x.astype(BF)
        out.append(part)
        x = x - part.astype(F32)
    return out


def dot_left(x, hot, count=3):
    return sum(dot(part, hot) for part in pieces(x, count))


def halves(a, b, part):
    lane = slice(part * HALF, (part + 1) * HALF)
    return jnp.concatenate([a[:, lane], b[:, lane]], axis=1)


def dot_stack(x, hot):
    both = dot(jnp.concatenate(pieces(x, 2), axis=0), hot)
    return both[: x.shape[0]] + both[x.shape[0] :]


def sweep(
    n,
    m,
    fa_hbm,
    p1_hbm,
    p2_hbm,
    p3_hbm,
    shrink_hbm,
    rows_ref,
    fine_ref,
    mid_ref,
    coarse_ref,
    spread_ref,
    fa_all,
    p1_all,
    p2_all,
    p3_ref,
    shrink_ref,
    rows_own,
    row_out,
    row_in,
    got,
    h1f,
    h2f,
    h1r,
    h1m,
    ht,
    hn,
    sums2,
    base1,
    pull1,
    scale2,
    part_own,
    part_all,
    cnt_own,
    cnt_all,
    cnt_third,
    cnt_top,
    means3,
    back_own,
    back_all,
    coarse_all,
    mid_half,
    fine_out,
    fine_in,
    fine_own,
    mid_own,
    coarse_own,
    err_own,
    err_all,
    tally,
    in_sem,
    id_send,
    id_recv,
    p2_send,
    p2_recv,
    row_send,
    row_recv,
    part_send,
    part_recv,
    cnt_send,
    cnt_recv,
    back_send,
    back_recv,
    coarse_recv,
    fine_send,
    fine_recv,
    mid_send,
    mid_recv,
    out_send,
    out_recv,
    err_send,
    err_recv,
    local_sem,
):
    me = lax.axis_index("clus")
    dp = lax.axis_index("dp")
    count, width = rows_ref.shape
    share = width // n
    tiles = share // LANES
    chunks = 2 * tiles
    fine_dev = p1_hbm.shape[1]
    middle = p2_hbm.shape[1]
    third = p3_hbm.shape[1]
    devices = n * m
    total = count * devices
    fine = n * fine_dev
    some = count // 2
    few = fine_dev // 2
    packed = n * some
    center_dp = m // 2 // 2 * 2
    pairs = m // 2
    pair = dp // 2
    side = lax.rem(dp, 2)
    near = (center_dp // 2 - 1, center_dp // 2)
    size = 4
    thin = HALF // size
    window = third // pairs
    mid_share = middle // n
    third_share = third // devices

    def span(index, size):
        return pl.ds(pl.multiple_of(index * size, size), size)

    def tile_of(t):
        return slice(t * LANES, (t + 1) * LANES)

    def column(index, t):
        return pl.ds(pl.multiple_of(index * share + t * LANES, LANES), LANES)

    def remote(src, dst, send, recv, device):
        return pltpu.make_async_remote_copy(
            src_ref=src,
            dst_ref=dst,
            send_sem=send,
            recv_sem=recv,
            device_id=device,
            device_id_type=MESH,
        )

    if n == 4:
        peers = [n - 1 - me, lax.rem(me + 2, n), me + 1 - 2 * lax.rem(me, 2)]
    else:
        peers = [lax.rem(me + k, n) for k in range(1, n)]

    def start(copies):
        for copy in copies:
            copy.start()

    def landed(ref, sem):
        pltpu.make_async_copy(ref, ref, sem).wait()

    low_half = pair < pairs // 2

    close = jnp.where(low_half, near[0], near[1])
    away = jnp.where(low_half, near[1], near[0])
    block = jnp.where(low_half, 2, 0)
    owners = (
        (away * 2, block),
        (away * 2 + 1, block + 1),
        (close * 2 + 1 - side, 2 - block + 1 - side),
        (close * 2 + side, 2 - block + side),
    )
    slot = owners[3][1]
    in_near = pair == close
    outer = [2 * chip + core for chip in range(pairs) if chip not in near for core in range(2)]

    def when_near(run):
        pl.when(in_near)(run)

    def when_outer(run):
        pl.when(jnp.logical_not(in_near))(run)

    def to_owners(do):
        for k in range(size - 1):
            do(k)
        when_outer(lambda: do(size - 1))

    if pairs == 4:
        inward = jnp.where(low_half, pair + 1, pair - 1)
        last = jnp.where(low_half, 3, 0)
        chips = [inward, 6 - pair - inward - last, last]
    else:
        chips = [lax.rem(pair + k, pairs) for k in range(1, pairs)]
    others = [chip * 2 + core for chip in reversed(chips) for core in range(2)]
    others.append(pair * 2 + 1 - side)

    barrier = pltpu.get_barrier_semaphore()
    for peer in peers:
        pl.semaphore_signal(barrier, inc=1, device_id={"clus": peer}, device_id_type=MESH)
    def greet(device):
        pl.semaphore_signal(barrier, inc=1, device_id={"dp": device}, device_id_type=MESH)

    to_owners(lambda k: greet(owners[k][0]))

    @when_near
    def _():
        for device in outer:
            greet(device)

    fetch = [
        pltpu.make_async_copy(src, dst, in_sem.at[i])
        for i, (src, dst) in enumerate(
            (
                (fa_hbm, fa_all.at[me]),
                (p1_hbm, p1_all.at[me]),
                (p2_hbm, p2_all.at[dp]),
                (rows_ref, rows_own),
                (p3_hbm, p3_ref),
                (shrink_hbm, shrink_ref),
            )
        )
    ]
    for copy in fetch:
        copy.start()
    pl.semaphore_wait(barrier, n - 1 + jnp.where(in_near, m - 1, size))
    for copy in fetch[:3]:
        copy.wait()

    for peer in peers:
        for which, ids in enumerate((fa_all, p1_all)):
            own = ids.at[me]
            start([remote(own, own, id_send.at[which], id_recv.at[which], {"clus": peer})])

    def p2_copy(k):
        own = p2_all.at[dp]
        return remote(own, own, p2_send, p2_recv, {"dp": owners[k][0]})

    to_owners(lambda k: p2_copy(k).start())
    fetch[3].wait()
    for q in range(chunks):
        t, a = divmod(q, 2)
        for p in range(n):
            lane = slice(p * share + t * LANES, p * share + (t + 1) * LANES)
            row_out[q, p] = halves(rows_own[0:some, lane], rows_own[some:count, lane], a)
        start(
            [
                remote(
                    row_out.at[q, peer],
                    row_in.at[q, span(me, some), :],
                    row_send,
                    row_recv.at[q],
                    {"clus": peer},
                )
                for peer in peers
            ]
        )
    for q in range(chunks):
        row_in[q, span(me, some), :] = row_out[q, me]

    for copy in fetch[4:]:
        copy.wait()
    w4 = shrink_ref[0] * (total / K4)
    w3 = shrink_ref[1] * (total / third)
    w2 = shrink_ref[2] * (total / (middle * m))
    w1 = shrink_ref[3] * (total / (fine_dev * devices))
    p3_row = p3_ref[...]
    upper = lax.broadcasted_iota(jnp.int32, (third, LANES), 1) >= K4
    h4 = jnp.where(upper, 1.0, lanes_hot(column_of(p3_row), 0).astype(F32)).astype(BF)
    h4f = rows_hot(LANES, p3_row)
    ones = jnp.ones((LANES, LANES), BF)

    def left_half(size):
        return lax.broadcasted_iota(jnp.int32, (size, LANES), 1) < HALF

    def parents_of(i):
        row = p2_all[i]
        ht[:, span(i, middle)] = rows_hot(third, row)
        p2_column = column_of(row)
        for j in range(0, third, LANES):
            hn[span(i, middle), j : j + LANES] = lanes_hot(p2_column, j)

    @when_near
    def _():
        parents_of(dp)

    landed(fa_all.at[0 : n - 1], id_recv.at[0])
    landed(p1_all.at[0 : n - 1], id_recv.at[1])
    ids = [fa_all[i] for i in range(n)]
    ids = [x[:, 0:some] for x in ids] + [x[:, some:count] for x in ids]
    fa_row = jnp.concatenate(ids, axis=1) - dp * fine
    table = [
        p1_all[i][:, j : j + LANES] for i in range(n) for j in range(0, fine_dev, LANES)
    ]
    table = (jnp.concatenate(table, axis=0) - dp * middle).astype(F32).astype(BF)
    line = fa_row // LANES
    picked = dot(table, rows_hot(LANES, fa_row - line * LANES))
    lines = lax.broadcasted_iota(jnp.int32, picked.shape, 0)
    mid_row = jnp.sum(jnp.where(lines == line, picked, 0.0), axis=0, keepdims=True)
    h2f[...] = rows_hot(middle, mid_row.astype(jnp.int32))

    def part_copy(q, k):
        device, o = owners[k]
        return remote(
            part_own.at[q, span(o, thin), :],
            part_all.at[q, dp],
            part_send,
            part_recv.at[q],
            {"dp": device},
        )

    def cnt_copy(k):
        place = {"dp": owners[k][0]}
        return remote(cnt_own, cnt_all.at[dp], cnt_send, cnt_recv, place)

    def sum_part(q):
        landed(row_in.at[q, 0 : (n - 1) * some], row_recv.at[q])
        block = row_in[q]
        both = jnp.where(
            left_half(middle), dot(h2f[:, 0:packed], block), dot(h2f[:, packed:], block)
        )
        both = both + pltpu.roll(both, HALF, 1)
        part_own[q] = both.T[0:HALF].astype(BF)
        to_owners(lambda k: part_copy(q, k).start())

        @when_near
        def _():
            part_all[q, dp] = part_own[q, span(slot, thin), :]

        sums2[q] = both

    count2 = h2f[:, 0:LANES]
    for j in range(LANES, n * count, LANES):
        count2 = count2 + h2f[:, j : j + LANES]
    count2 = dot(count2, ones)
    cnt_own[...] = count2.T[0:1]
    to_owners(lambda k: cnt_copy(k).start())
    cnt_all[dp] = cnt_own[...]
    sum_part(0)
    @when_near
    def _():
        landed(p2_all.at[0 : m - 1], p2_recv)
        for i in others:
            parents_of(i)


    def back_copy(q, k):
        peer = others[k]
        return remote(
            back_own.at[q, :, span(peer, middle)],
            back_all.at[q, span(slot, thin), :],
            back_send.at[0],
            back_recv.at[q],
            {"dp": peer},
        )

    def coarse_copy(q, k):
        peer = others[k]
        return remote(
            means3.at[q, :, span(peer // 2, window)],
            coarse_all.at[q, span(slot, thin), :],
            back_send.at[1],
            coarse_recv.at[q // 2],
            {"dp": peer},
        )

    def from_owners(ref, sem):
        when_near(lambda: landed(ref.at[:, 0 : (size - 1) * thin], sem))
        when_outer(lambda: landed(ref, sem))

    def third_counts():
        landed(cnt_all.at[0 : m - 1], cnt_recv)
        lines = jnp.concatenate([cnt_all[i] for i in range(m)], axis=1)
        row = lax.broadcasted_iota(jnp.int32, (16, m * middle), 0)
        stack = jnp.zeros((16, m * middle), F32)
        for i, part in enumerate(pieces(lines, 3)):
            stack = jnp.where(row == i, part.astype(F32), stack)
        cnt3 = dot(stack.astype(BF), hn[...])
        cnt3 = cnt3[0:1] + cnt3[1:2] + cnt3[2:3]
        cnt_third[...] = cnt3
        cnt_top[...] = dot_stack(jnp.broadcast_to(cnt3, (16, third)), h4)[0:1]

    def third_level(q):
        landed(part_all.at[q, 0 : m - 1], part_recv.at[q])
        sums3 = dot(jnp.concatenate([part_all[q, i] for i in range(m)], axis=1), hn[...])
        sums4 = dot_stack(sums3, h4)
        cnt3, cnt4 = cnt_third[...], cnt_top[...]
        center = pltpu.roll(sums4, K4, 1) / total
        means4 = (sums4 + w4 * center) / (cnt4 + w4)
        block = ((sums3 + w3 * dot_stack(means4, h4f)) / (cnt3 + w3)).astype(BF)
        means3[q] = block
        back_own[q] = dot(block, ht[...]).astype(BF)
        for k in range(m - 1):
            back_copy(q, k).start()
        for k in range(m - 1):
            coarse_copy(q, k).start()
        back_all[q, span(slot, thin), :] = back_own[q, :, span(dp, middle)]
        coarse_all[q, span(slot, thin), :] = means3[q, :, span(dp // 2, window)]

    def run_third(q):
        when_near(lambda: third_level(q))

    def unpack(t):
        a, b = row_in[2 * t], row_in[2 * t + 1]
        got[0:packed, tile_of(t)] = halves(a, b, 0)
        got[packed:, tile_of(t)] = halves(a, b, 1)

    def fine_counts():
        some_counts = h1f[:, 0:LANES]
        for j in range(LANES, n * count, LANES):
            some_counts = some_counts + h1f[:, j : j + LANES]
        return dot(some_counts, ones)

    def bases():
        for t in range(tiles):
            unpack(t)
        left = left_half(few)
        scale2[...] = 1.0 / (count2 + w2)
        rate1 = 1.0 / (fine_counts() + w1)
        sums1 = dot(h1f[...], got[...])
        for p in range(n):
            low = slice(p * fine_dev, p * fine_dev + few)
            high = slice(p * fine_dev + few, (p + 1) * fine_dev)
            place = slice(p * few, (p + 1) * few)
            pull1[place, :] = w1 * jnp.where(left, rate1[low], rate1[high])
            for t in range(tiles):
                a = sums1[low, tile_of(t)] * rate1[low]
                b = sums1[high, tile_of(t)] * rate1[high]
                base1[2 * t, place, :] = halves(a, b, 0)
                base1[2 * t + 1, place, :] = halves(a, b, 1)

    def down(q):
        t, a = divmod(q, 2)
        from_owners(back_all.at[q : q + 1], back_recv.at[q])
        prior2 = back_all[q].astype(F32)
        prior2 = jnp.concatenate([prior2, prior2], axis=0).T
        means2 = (sums2[q] + w2 * prior2) * scale2[...]
        prior1 = sum(dot(h1m[...], part) for part in pieces(means2, 2))
        left = left_half(few)
        for p in range(n):
            low = prior1[p * fine_dev : p * fine_dev + few]
            high = prior1[p * fine_dev + few : (p + 1) * fine_dev]
            place = slice(p * few, (p + 1) * few)
            means1 = base1[q, place] + pull1[place] * jnp.where(left, low, high)
            fine_out[q, p] = means1.astype(BF)
        start(
            [
                remote(
                    fine_out.at[q, peer],
                    fine_in.at[q, me],
                    fine_send,
                    fine_recv.at[t],
                    {"clus": peer},
                )
                for k, peer in enumerate(peers)
            ]
        )
        if not a:
            mid_half[...] = means2
            return
        mid_own[:, tile_of(t)] = jnp.where(left_half(middle), mid_half[...], means2).astype(BF)
        start(
            [
                remote(
                    mid_own.at[span(peer, mid_share), tile_of(t)],
                    mid_ref.at[:, column(me, t)],
                    mid_send,
                    mid_recv,
                    {"clus": peer},
                )
                for peer in peers
            ]
        )
        copy = pltpu.make_async_copy(
            mid_own.at[span(me, mid_share), tile_of(t)], mid_ref.at[:, column(me, t)], local_sem.at[0]
        )
        copy.start()

    def rows_by_fine():
        fa_column = column_of(fa_row)
        for j in range(0, fine, LANES):
            h1r[:, j : j + LANES] = lanes_hot(fa_column, j)

    def coarse(t):
        from_owners(coarse_all.at[2 * t : 2 * t + 2], coarse_recv.at[t])
        block = jnp.concatenate([coarse_all[2 * t], coarse_all[2 * t + 1]], axis=0)
        coarse_own[:, tile_of(t)] = block.astype(F32).T.astype(BF)

        def place(peer):
            return coarse_own.at[span(side * n + peer, third_share), tile_of(t)]

        start(
            [
                remote(
                    place(peer), coarse_ref.at[:, column(me, t)], out_send, out_recv, {"clus": peer}
                )
                for peer in peers
            ]
        )
        copy = pltpu.make_async_copy(place(me), coarse_ref.at[:, column(me, t)], local_sem.at[1])
        copy.start()

    def fine_tile(t):
        for p in range(n):
            a, b = fine_out[2 * t, p], fine_out[2 * t + 1, p]
            fine_own[p * fine_dev : p * fine_dev + few, tile_of(t)] = halves(a, b, 0)
            fine_own[p * fine_dev + few : (p + 1) * fine_dev, tile_of(t)] = halves(a, b, 1)

    p1_row = jnp.concatenate([p1_all[i] for i in range(n)], axis=1) - dp * middle
    p1_column = column_of(p1_row)
    for j in range(0, middle, LANES):
        h1m[:, j : j + LANES] = lanes_hot(p1_column, j)
    sum_part(1)
    h1f[...] = rows_hot(fine, fa_row)
    for q in range(2, chunks - 1):
        sum_part(q)
    when_near(third_counts)
    run_third(0)
    sum_part(chunks - 1)
    run_third(1)
    bases()
    run_third(2)
    down(0)
    for q in range(3, chunks):
        run_third(q)
    for q in range(1, chunks):
        down(q)
        if q % 2 and q < chunks - 1:
            coarse(q // 2)
            fine_tile(q // 2)
            rows_by_fine()
    if chunks == 2:
        rows_by_fine()
    coarse(tiles - 1)
    fine_tile(tiles - 1)
    fine_ref[:, span(me, share)] = fine_own[span(me, fine_dev), :]
    diff = got[...].astype(F32) - dot(h1r[...], fine_own[...])
    square = diff * diff
    folded = square[:, :LANES]
    for j in range(LANES, share, LANES):
        folded = folded + square[:, j : j + LANES]
    square = folded
    err_row = jnp.sum(square.T, axis=0, keepdims=True)
    parts = pieces(err_row, 3)
    line = lax.broadcasted_iota(jnp.int32, (16, n * count), 0)
    stack = jnp.where(line == 3, 1.0, 0.0)
    for i, part in enumerate(parts):
        stack = jnp.where(line == i, part.astype(F32), stack)
    by_fine = dot(stack.astype(BF), h1r[...])
    err_fine = by_fine[0:1] + by_fine[1:2] + by_fine[2:3]
    for i in range(n):
        err_own[i] = err_fine[:, i * fine_dev : (i + 1) * fine_dev]
        tally[i] = by_fine[3:4, i * fine_dev : (i + 1) * fine_dev]
    start(
        [
            remote(err_own.at[peer], err_all.at[me], err_send, err_recv, {"clus": peer})
            for peer in peers
        ]
    )
    err_all[me] = err_own[me]

    for t in range(tiles):
        landed(fine_in.at[2 * t : 2 * t + 2, 0 : n - 1], fine_recv.at[t])
        for k in range(1, n):
            peer = lax.rem(me + k, n)
            a, b = fine_in[2 * t, peer], fine_in[2 * t + 1, peer]
            fine_ref[0:few, column(peer, t)] = halves(a, b, 0)
            fine_ref[few:, column(peer, t)] = halves(a, b, 1)
    landed(err_all.at[0 : n - 1], err_recv)
    err = err_all[0]
    for i in range(1, n):
        err = err + err_all[i]
    spread_ref[...] = err / (width * (tally[me] + 1.0))
    landed(mid_ref.at[:, 0:share], local_sem.at[0])
    landed(coarse_ref.at[:, 0:share], local_sem.at[1])
    landed(mid_ref.at[:, 0 : (n - 1) * share], mid_recv)
    landed(coarse_ref.at[:, 0 : (n - 1) * share], out_recv)
    landed(fa_all.at[0 : n - 1], id_send.at[0])
    landed(p1_all.at[0 : n - 1], id_send.at[1])
    landed(row_out.at[:, 0 : n - 1], row_send)
    landed(fine_out.at[:, 0 : n - 1], fine_send)
    landed(mid_own.at[0 : (n - 1) * mid_share], mid_send)
    landed(coarse_own.at[0 : (n - 1) * third_share], out_send)
    landed(err_own.at[0 : n - 1], err_send)

    @when_outer
    def _():
        landed(p2_all.at[0:size], p2_send)
        landed(cnt_all.at[0:size], cnt_send)
        landed(part_own, part_send)

    @when_near
    def _():
        landed(p2_all.at[0 : size - 1], p2_send)
        landed(cnt_all.at[0 : size - 1], cnt_send)
        landed(part_own.at[:, 0 : (size - 1) * thin], part_send)
        landed(back_own.at[:, :, 0 : (m - 1) * middle], back_send.at[0])
        landed(back_own.at[:, :, 0 : (m - 1) * window], back_send.at[1])


def land(count, *refs):
    sem = refs[-1]
    pairs = zip(refs[:count], refs[count : 2 * count])
    copies = [pltpu.make_async_copy(a, b, sem.at[i]) for i, (a, b) in enumerate(pairs)]
    for copy in copies:
        copy.start()
    for copy in copies:
        copy.wait()


def settle(*arrays):
    count = len(arrays)
    return pl.pallas_call(
        functools.partial(land, count),
        out_shape=tuple(jax.ShapeDtypeStruct(a.shape, a.dtype) for a in arrays),
        in_specs=[pl.BlockSpec(memory_space=pltpu.VMEM)] * count,
        out_specs=tuple([pl.BlockSpec(memory_space=pl.ANY)] * count),
        scratch_shapes=[pltpu.SemaphoreType.DMA((count,))],
        compiler_params=pltpu.CompilerParams(vmem_limit_bytes=4 << 20),
        name="settle",
    )(*arrays)


def fused(rows, fine_assign, parent1, parent2, parent3, shrink):
    n = lax.axis_size("clus")
    m = lax.axis_size("dp")
    count, width = rows.shape
    fine_dev = parent1.shape[0]
    middle = parent2.shape[0]
    third = parent3.shape[0]
    share = width // n
    tiles = share // LANES
    chunks = 2 * tiles
    window = third // (m // 2)
    fine = n * fine_dev
    total_rows = n * count
    vmem = pl.BlockSpec(memory_space=pltpu.VMEM)
    hbm = pl.BlockSpec(memory_space=pltpu.HBM)
    dma = pltpu.SemaphoreType.DMA

    def stay(x):
        return pltpu.with_memory_space_constraint(x, pltpu.HBM)

    fine_out, mid_out, coarse_out, spread = pl.pallas_call(
        functools.partial(sweep, n, m),
        out_shape=(
            jax.ShapeDtypeStruct((fine_dev, width), BF),
            jax.ShapeDtypeStruct((middle // n, width), BF),
            jax.ShapeDtypeStruct((third // (n * m), width), BF),
            jax.ShapeDtypeStruct((1, fine_dev), F32),
        ),
        in_specs=[hbm] * 6,
        out_specs=[vmem] * 4,
        scratch_shapes=[
            pltpu.VMEM((n, 1, count), jnp.int32),
            pltpu.VMEM((n, 1, fine_dev), jnp.int32),
            pltpu.VMEM((m, 1, middle), jnp.int32),
            pltpu.VMEM((1, third), jnp.int32),
            pltpu.SMEM((4,), F32),
            pltpu.VMEM((count, width), BF),
            pltpu.VMEM((chunks, n, count // 2, LANES), BF),
            pltpu.VMEM((chunks, total_rows // 2, LANES), BF),
            pltpu.VMEM((total_rows, share), BF),
            pltpu.VMEM((fine, total_rows), BF),
            pltpu.VMEM((middle, total_rows), BF),
            pltpu.VMEM((total_rows, fine), BF),
            pltpu.VMEM((fine, middle), BF),
            pltpu.VMEM((third, m * middle), BF),
            pltpu.VMEM((m * middle, third), BF),
            pltpu.VMEM((chunks, middle, LANES), F32),
            pltpu.VMEM((chunks, fine // 2, LANES), F32),
            pltpu.VMEM((fine // 2, LANES), F32),
            pltpu.VMEM((middle, LANES), F32),
            pltpu.VMEM((chunks, HALF, middle), BF),
            pltpu.VMEM((chunks, m, HALF // 4, middle), BF),
            pltpu.VMEM((1, middle), F32),
            pltpu.VMEM((m, 1, middle), F32),
            pltpu.VMEM((1, third), F32),
            pltpu.VMEM((1, LANES), F32),
            pltpu.VMEM((chunks, HALF // 4, third), BF),
            pltpu.VMEM((chunks, HALF // 4, m * middle), BF),
            pltpu.VMEM((chunks, HALF, middle), BF),
            pltpu.VMEM((chunks, HALF, window), BF),
            pltpu.VMEM((middle, LANES), F32),
            pltpu.VMEM((chunks, n, fine_dev // 2, LANES), BF),
            pltpu.VMEM((chunks, n, fine_dev // 2, LANES), BF),
            pltpu.VMEM((fine, share), BF),
            pltpu.VMEM((middle, share), BF),
            pltpu.VMEM((window, share), BF),
            pltpu.VMEM((n, 1, fine_dev), F32),
            pltpu.VMEM((n, 1, fine_dev), F32),
            pltpu.VMEM((n, 1, fine_dev), F32),
            dma((6,)),
            dma((2,)),
            dma((2,)),
            dma,
            dma,
            dma,
            dma((chunks,)),
            dma,
            dma((chunks,)),
            dma,
            dma,
            dma((2,)),
            dma((chunks,)),
            dma((tiles,)),
            dma,
            dma((tiles,)),
            dma,
            dma,
            dma,
            dma,
            dma,
            dma,
            dma((2,)),
        ],
        compiler_params=pltpu.CompilerParams(
            collective_id=0, has_side_effects=True, vmem_limit_bytes=40 << 20
        ),
        name="sweep",
    )(
        stay(fine_assign.reshape(1, count)),
        stay(parent1.reshape(1, fine_dev)),
        stay(parent2.reshape(1, middle)),
        stay(parent3.reshape(1, third)),
        stay(shrink),
        stay(rows),
    )
    fine_out, mid_out, coarse_out, spread = settle(fine_out, mid_out, coarse_out, spread)
    return fine_out, mid_out, coarse_out, spread.reshape(fine_dev)


def fits(rows, fine_assign, parent1, parent2, parent3):
    n = lax.axis_size("clus")
    m = lax.axis_size("dp")
    return (
        rows.shape[1] == 2 * n * LANES
        and m % 4 == 0
        and rows.shape[0] % (2 * LANES) == 0
        and parent1.shape[0] % (2 * LANES) == 0
        and parent2.shape[0] % LANES == 0
        and parent2.shape[0] <= 256
        and parent2.shape[0] % (n * 16) == 0
        and parent3.shape[0] % (m // 2 * LANES) == 0
        and parent3.shape[0] // (m // 2) <= parent2.shape[0]
        and parent3.shape[0] % (n * m * 16) == 0
    )


def step(rows, fine_assign, parent1, parent2, parent3, shrink):
    form = fused if fits(rows, fine_assign, parent1, parent2, parent3) else local
    return form(rows, fine_assign, parent1, parent2, parent3, shrink)


def solution(mesh):
    placed = (P(("dp", "clus"), None), P(("dp", "clus")), P(("dp", "clus")), P("dp"), P(), P())
    return jax.shard_map(
        step,
        mesh=mesh,
        in_specs=placed,
        out_specs=(
            P(("dp", "clus"), None),
            P(("dp", "clus"), None),
            P(("dp", "clus"), None),
            P(("dp", "clus")),
        ),
        check_vma=False,
    )
```

```python
import functools

import jax
import jax.numpy as jnp
from jax import lax
from jax.experimental import pallas as pl
from jax.experimental.pallas import tpu as pltpu
from jax.sharding import PartitionSpec as P

K4 = 64


HIGH = lax.Precision.HIGHEST


def shrunk(sums, counts, prior, weight):
    return (sums + weight * prior) / (counts + weight)[:, None]


def local(rows, fine_assign, parent1, parent2, parent3, shrink):
    groups = lax.axis_size("clus")
    dp_count = lax.axis_size("dp")
    devices = groups * dp_count
    clus_index = lax.axis_index("clus")
    dp_index = lax.axis_index("dp")
    count = rows.shape[0]
    width = rows.shape[1]
    fine_dev = parent1.shape[0]
    middle_dp = parent2.shape[0]
    third = parent3.shape[0]
    slots = 2 * count // groups
    total = count * devices
    weight_top = shrink[0] * (total / K4)
    weight_third = shrink[1] * (total / third)
    weight_middle = shrink[2] * (total / (middle_dp * dp_count))
    weight_fine = shrink[3] * (total / (fine_dev * devices))
    local_ids = fine_assign - dp_index * groups * fine_dev
    target = local_ids // fine_dev
    within = local_ids - target * fine_dev
    target_hot = (target[:, None] == jnp.arange(groups)[None, :]).astype(jnp.bfloat16)
    earlier = (jnp.arange(count)[:, None] > jnp.arange(count)[None, :]).astype(jnp.bfloat16)
    before = jnp.dot(earlier, target_hot, preferred_element_type=jnp.float32)
    rank = jnp.sum(before * target_hot.astype(jnp.float32), axis=1).astype(jnp.int32)
    slot_of = target * slots + rank
    source = (
        jnp.full((groups * slots,), count, jnp.int32)
        .at[slot_of]
        .set(jnp.arange(count, dtype=jnp.int32))
    )
    padded = jnp.concatenate([rows, jnp.zeros((1, width), jnp.bfloat16)], axis=0)
    send_rows = padded[source].reshape(groups, slots, width)
    send_ids = jnp.concatenate([within, jnp.full((1,), -1, jnp.int32)])[source].reshape(
        groups, slots
    )
    got_rows, got_ids = (
        lax.all_to_all(send_rows, "clus", split_axis=0, concat_axis=0, tiled=True),
        lax.all_to_all(send_ids, "clus", split_axis=0, concat_axis=0, tiled=True),
    )
    got_rows = got_rows.reshape(groups * slots, width)
    got_ids = got_ids.reshape(groups * slots)
    member = (got_ids[:, None] == jnp.arange(fine_dev)[None, :]).astype(jnp.bfloat16)
    contract = (((0,), (0,)), ((), ()))
    fine_sums = lax.dot_general(member, got_rows, contract, preferred_element_type=jnp.float32)
    fine_counts = jnp.sum(member.astype(jnp.float32), axis=0)
    middle_local = parent1 - dp_index * middle_dp
    child_hot = (jnp.arange(middle_dp)[:, None] == middle_local[None, :]).astype(jnp.float32)
    middle_part = jnp.dot(child_hot, fine_sums, precision=HIGH)
    middle_tally = jnp.dot(child_hot, fine_counts, precision=HIGH)
    share = middle_dp // groups
    offset = clus_index * share
    middle_sums, middle_counts = (
        lax.psum_scatter(middle_part, "clus", scatter_dimension=0, tiled=True),
        lax.psum_scatter(middle_tally, "clus", scatter_dimension=0, tiled=True),
    )
    own_parent2 = lax.dynamic_slice_in_dim(parent2, offset, share, 0)
    third_share = third // devices
    third_start = (dp_index * groups + clus_index) * third_share
    third_hot = (jnp.arange(third)[:, None] == own_parent2[None, :]).astype(jnp.float32)
    third_part = jnp.dot(third_hot, middle_sums, precision=HIGH)
    third_tally = jnp.dot(third_hot, middle_counts, precision=HIGH)
    third_sums, third_counts = lax.psum((third_part, third_tally), ("dp", "clus"))
    top_hot = (jnp.arange(K4)[:, None] == parent3[None, :]).astype(jnp.float32)
    top_sums = jnp.dot(top_hot, third_sums, precision=HIGH)
    top_counts = jnp.dot(top_hot, third_counts, precision=HIGH)
    center = jnp.sum(top_sums, axis=0) / total
    top_means = shrunk(top_sums, top_counts, center[None, :], weight_top)
    third_means = shrunk(
        third_sums, third_counts, jnp.dot(top_hot.T, top_means, precision=HIGH), weight_third
    )
    third_out = lax.dynamic_slice_in_dim(third_means, third_start, third_share, 0)
    parent_hot = (own_parent2[:, None] == jnp.arange(third)[None, :]).astype(jnp.float32)
    middle_out = shrunk(
        middle_sums, middle_counts, jnp.dot(parent_hot, third_means, precision=HIGH), weight_middle
    )
    middle_means = lax.all_gather(middle_out, "clus", axis=0, tiled=True)
    fine_means = shrunk(
        fine_sums, fine_counts, jnp.dot(child_hot.T, middle_means, precision=HIGH), weight_fine
    )
    fine_out = fine_means.astype(jnp.bfloat16)
    back = jnp.dot(member, fine_out, preferred_element_type=jnp.float32)
    diff = got_rows.astype(jnp.float32) - back
    row_error = jnp.sum(diff * diff, axis=1)
    spread = jnp.sum(member.astype(jnp.float32) * row_error[:, None], axis=0) / (
        width * (fine_counts + 1.0)
    )
    return (fine_out, middle_out.astype(jnp.bfloat16), third_out.astype(jnp.bfloat16), spread)


LANES = 128
HALF = LANES // 2
BF = jnp.bfloat16
F32 = jnp.float32
MESH = pl.DeviceIdType.MESH


def rows_hot(size, ids):
    shape = (size, ids.shape[1])
    lines = lax.broadcasted_iota(jnp.int16, shape, 0)
    same = lines == jnp.broadcast_to(ids.astype(jnp.int16), shape)
    return jnp.where(same, jnp.ones(shape, BF), jnp.zeros(shape, BF))


def column_of(ids):
    column = jnp.broadcast_to(ids.astype(F32), (LANES, ids.shape[1])).T
    return column.astype(jnp.int32).astype(jnp.int16)


def lanes_hot(column, start):
    shape = column.shape
    same = column == lax.broadcasted_iota(jnp.int16, shape, 1) + jnp.int16(start)
    return jnp.where(same, jnp.ones(shape, BF), jnp.zeros(shape, BF))


def dot(a, b):
    return jnp.dot(a, b, preferred_element_type=F32)


def pieces(x, count):
    out = []
    for _ in range(count):
        part = x.astype(BF)
        out.append(part)
        x = x - part.astype(F32)
    return out


def dot_left(x, hot, count=3):
    return sum(dot(part, hot) for part in pieces(x, count))


def halves(a, b, part):
    lane = slice(part * HALF, (part + 1) * HALF)
    return jnp.concatenate([a[:, lane], b[:, lane]], axis=1)


def dot_stack(x, hot):
    both = dot(jnp.concatenate(pieces(x, 2), axis=0), hot)
    return both[: x.shape[0]] + both[x.shape[0] :]


def sweep(
    n,
    m,
    fa_hbm,
    p1_hbm,
    p2_hbm,
    p3_hbm,
    shrink_hbm,
    rows_ref,
    fine_ref,
    mid_ref,
    coarse_ref,
    spread_ref,
    fa_all,
    p1_all,
    p2_all,
    p3_ref,
    shrink_ref,
    rows_own,
    row_out,
    row_in,
    got,
    h1f,
    h2f,
    h1r,
    h1m,
    ht,
    hn,
    sums2,
    base1,
    pull1,
    scale2,
    rate1,
    part_own,
    part_all,
    cnt_own,
    cnt_all,
    cnt_third,
    cnt_top,
    means3,
    back_own,
    back_all,
    coarse_all,
    mid_half,
    fine_out,
    fine_in,
    fine_own,
    mid_own,
    coarse_own,
    err_own,
    err_all,
    tally,
    in_sem,
    id_send,
    id_recv,
    p2_send,
    p2_recv,
    row_send,
    row_recv,
    part_send,
    part_recv,
    cnt_send,
    cnt_recv,
    back_send,
    back_recv,
    coarse_recv,
    fine_send,
    fine_recv,
    mid_send,
    mid_recv,
    out_send,
    out_recv,
    err_send,
    err_recv,
    local_sem,
):
    me = lax.axis_index("clus")
    dp = lax.axis_index("dp")
    count, width = rows_ref.shape
    share = width // n
    tiles = share // LANES
    chunks = 2 * tiles
    fine_dev = p1_hbm.shape[1]
    middle = p2_hbm.shape[1]
    third = p3_hbm.shape[1]
    devices = n * m
    total = count * devices
    fine = n * fine_dev
    some = count // 2
    few = fine_dev // 2
    packed = n * some
    center_dp = m // 2 // 2 * 2
    pairs = m // 2
    pair = dp // 2
    side = lax.rem(dp, 2)
    near = (center_dp // 2 - 1, center_dp // 2)
    size = 4
    thin = HALF // size
    window = third // pairs
    mid_share = middle // n
    third_share = third // devices

    def span(index, size):
        return pl.ds(pl.multiple_of(index * size, size), size)

    def tile_of(t):
        return slice(t * LANES, (t + 1) * LANES)

    def column(index, t):
        return pl.ds(pl.multiple_of(index * share + t * LANES, LANES), LANES)

    def remote(src, dst, send, recv, device):
        return pltpu.make_async_remote_copy(
            src_ref=src,
            dst_ref=dst,
            send_sem=send,
            recv_sem=recv,
            device_id=device,
            device_id_type=MESH,
        )

    if n == 4:
        peers = [n - 1 - me, lax.rem(me + 2, n), me + 1 - 2 * lax.rem(me, 2)]
    else:
        peers = [lax.rem(me + k, n) for k in range(1, n)]

    def start(copies):
        for copy in copies:
            copy.start()

    def landed(ref, sem):
        pltpu.make_async_copy(ref, ref, sem).wait()

    low_half = pair < pairs // 2

    close = jnp.where(low_half, near[0], near[1])
    away = jnp.where(low_half, near[1], near[0])
    block = jnp.where(low_half, 2, 0)
    owners = (
        (away * 2, block),
        (away * 2 + 1, block + 1),
        (close * 2 + 1 - side, 2 - block + 1 - side),
        (close * 2 + side, 2 - block + side),
    )
    slot = owners[3][1]
    in_near = pair == close
    outer = [2 * chip + core for chip in range(pairs) if chip not in near for core in range(2)]

    def when_near(run):
        pl.when(in_near)(run)

    def when_outer(run):
        pl.when(jnp.logical_not(in_near))(run)

    def to_owners(do):
        for k in range(size - 1):
            do(k)
        when_outer(lambda: do(size - 1))

    if pairs == 4:
        inward = jnp.where(low_half, pair + 1, pair - 1)
        last = jnp.where(low_half, 3, 0)
        chips = [inward, 6 - pair - inward - last, last]
    else:
        chips = [lax.rem(pair + k, pairs) for k in range(1, pairs)]
    others = [chip * 2 + core for chip in reversed(chips) for core in range(2)]
    others.append(pair * 2 + 1 - side)

    barrier = pltpu.get_barrier_semaphore()
    for peer in peers:
        pl.semaphore_signal(barrier, inc=1, device_id={"clus": peer}, device_id_type=MESH)
    def greet(device):
        pl.semaphore_signal(barrier, inc=1, device_id={"dp": device}, device_id_type=MESH)

    to_owners(lambda k: greet(owners[k][0]))

    @when_near
    def _():
        for device in outer:
            greet(device)

    fetch = [
        pltpu.make_async_copy(src, dst, in_sem.at[i])
        for i, (src, dst) in enumerate(
            (
                (fa_hbm, fa_all.at[me]),
                (p1_hbm, p1_all.at[me]),
                (p2_hbm, p2_all.at[dp]),
                (rows_ref, rows_own),
                (p3_hbm, p3_ref),
                (shrink_hbm, shrink_ref),
            )
        )
    ]
    for copy in fetch:
        copy.start()
    pl.semaphore_wait(barrier, n - 1 + jnp.where(in_near, m - 1, size))
    for copy in fetch[:3]:
        copy.wait()

    for peer in peers:
        for which, ids in enumerate((fa_all, p1_all)):
            own = ids.at[me]
            start([remote(own, own, id_send.at[which], id_recv.at[which], {"clus": peer})])

    def p2_copy(k):
        own = p2_all.at[dp]
        return remote(own, own, p2_send, p2_recv, {"dp": owners[k][0]})

    to_owners(lambda k: p2_copy(k).start())
    fetch[3].wait()
    for q in range(chunks):
        t, a = divmod(q, 2)
        for p in range(n):
            lane = slice(p * share + t * LANES, p * share + (t + 1) * LANES)
            row_out[q, p] = halves(rows_own[0:some, lane], rows_own[some:count, lane], a)
        start(
            [
                remote(
                    row_out.at[q, peer],
                    row_in.at[q, span(me, some), :],
                    row_send,
                    row_recv.at[q],
                    {"clus": peer},
                )
                for peer in peers
            ]
        )
    for q in range(chunks):
        row_in[q, span(me, some), :] = row_out[q, me]

    for copy in fetch[4:]:
        copy.wait()
    w4 = shrink_ref[0] * (total / K4)
    w3 = shrink_ref[1] * (total / third)
    w2 = shrink_ref[2] * (total / (middle * m))
    w1 = shrink_ref[3] * (total / (fine_dev * devices))
    p3_row = p3_ref[...]
    upper = lax.broadcasted_iota(jnp.int32, (third, LANES), 1) >= K4
    h4 = jnp.where(upper, 1.0, lanes_hot(column_of(p3_row), 0).astype(F32)).astype(BF)
    h4f = rows_hot(LANES, p3_row)
    ones = jnp.ones((LANES, LANES), BF)

    def left_half(size):
        return lax.broadcasted_iota(jnp.int32, (size, LANES), 1) < HALF

    def parents_of(i):
        row = p2_all[i]
        ht[:, span(i, middle)] = rows_hot(third, row)
        p2_column = column_of(row)
        for j in range(0, third, LANES):
            hn[span(i, middle), j : j + LANES] = lanes_hot(p2_column, j)

    @when_near
    def _():
        parents_of(dp)

    landed(fa_all.at[0 : n - 1], id_recv.at[0])
    landed(p1_all.at[0 : n - 1], id_recv.at[1])
    ids = [fa_all[i] for i in range(n)]
    ids = [x[:, 0:some] for x in ids] + [x[:, some:count] for x in ids]
    fa_row = jnp.concatenate(ids, axis=1) - dp * fine
    table = [
        p1_all[i][:, j : j + LANES] for i in range(n) for j in range(0, fine_dev, LANES)
    ]
    table = (jnp.concatenate(table, axis=0) - dp * middle).astype(F32).astype(BF)
    line = fa_row // LANES
    picked = dot(table, rows_hot(LANES, fa_row - line * LANES))
    lines = lax.broadcasted_iota(jnp.int32, picked.shape, 0)
    mid_row = jnp.sum(jnp.where(lines == line, picked, 0.0), axis=0, keepdims=True)
    h2f[...] = rows_hot(middle, mid_row.astype(jnp.int32))

    def part_copy(q, k):
        device, o = owners[k]
        return remote(
            part_own.at[q, span(o, thin), :],
            part_all.at[q, dp],
            part_send,
            part_recv.at[q],
            {"dp": device},
        )

    def cnt_copy(k):
        place = {"dp": owners[k][0]}
        return remote(cnt_own, cnt_all.at[dp], cnt_send, cnt_recv, place)

    def sum_part(q):
        landed(row_in.at[q, 0 : (n - 1) * some], row_recv.at[q])
        block = row_in[q]
        both = jnp.where(
            left_half(middle), dot(h2f[:, 0:packed], block), dot(h2f[:, packed:], block)
        )
        both = both + pltpu.roll(both, HALF, 1)
        part_own[q] = both.T[0:HALF].astype(BF)
        to_owners(lambda k: part_copy(q, k).start())

        @when_near
        def _():
            part_all[q, dp] = part_own[q, span(slot, thin), :]

        sums2[q] = both

    count2 = h2f[:, 0:LANES]
    for j in range(LANES, n * count, LANES):
        count2 = count2 + h2f[:, j : j + LANES]
    count2 = dot(count2, ones)
    cnt_own[...] = count2.T[0:1]
    to_owners(lambda k: cnt_copy(k).start())
    cnt_all[dp] = cnt_own[...]
    sum_part(0)
    @when_near
    def _():
        landed(p2_all.at[0 : m - 1], p2_recv)
        for i in others:
            parents_of(i)


    def back_copy(q, k):
        peer = others[k]
        return remote(
            back_own.at[q, :, span(peer, middle)],
            back_all.at[q, span(slot, thin), :],
            back_send.at[0],
            back_recv.at[q],
            {"dp": peer},
        )

    def coarse_copy(q, k):
        peer = others[k]
        return remote(
            means3.at[q, :, span(peer // 2, window)],
            coarse_all.at[q, span(slot, thin), :],
            back_send.at[1],
            coarse_recv.at[q // 2],
            {"dp": peer},
        )

    def from_owners(ref, sem):
        when_near(lambda: landed(ref.at[:, 0 : (size - 1) * thin], sem))
        when_outer(lambda: landed(ref, sem))

    def third_counts():
        landed(cnt_all.at[0 : m - 1], cnt_recv)
        lines = jnp.concatenate([cnt_all[i] for i in range(m)], axis=1)
        row = lax.broadcasted_iota(jnp.int32, (16, m * middle), 0)
        stack = jnp.zeros((16, m * middle), F32)
        for i, part in enumerate(pieces(lines, 3)):
            stack = jnp.where(row == i, part.astype(F32), stack)
        cnt3 = dot(stack.astype(BF), hn[...])
        cnt3 = cnt3[0:1] + cnt3[1:2] + cnt3[2:3]
        cnt_third[...] = cnt3
        cnt_top[...] = dot_stack(jnp.broadcast_to(cnt3, (16, third)), h4)[0:1]

    def third_level(q):
        landed(part_all.at[q, 0 : m - 1], part_recv.at[q])
        sums3 = dot(jnp.concatenate([part_all[q, i] for i in range(m)], axis=1), hn[...])
        sums4 = dot_stack(sums3, h4)
        cnt3, cnt4 = cnt_third[...], cnt_top[...]
        center = pltpu.roll(sums4, K4, 1) / total
        means4 = (sums4 + w4 * center) / (cnt4 + w4)
        block = ((sums3 + w3 * dot_stack(means4, h4f)) / (cnt3 + w3)).astype(BF)
        means3[q] = block
        back_own[q] = dot(block, ht[...]).astype(BF)
        for k in range(m - 1):
            back_copy(q, k).start()
        for k in range(m - 1):
            coarse_copy(q, k).start()
        back_all[q, span(slot, thin), :] = back_own[q, :, span(dp, middle)]
        coarse_all[q, span(slot, thin), :] = means3[q, :, span(dp // 2, window)]

    def run_third(q):
        when_near(lambda: third_level(q))

    def unpack(t):
        a, b = row_in[2 * t], row_in[2 * t + 1]
        got[0:packed, tile_of(t)] = halves(a, b, 0)
        got[packed:, tile_of(t)] = halves(a, b, 1)

    def fine_counts():
        some_counts = h1f[:, 0:LANES]
        for j in range(LANES, n * count, LANES):
            some_counts = some_counts + h1f[:, j : j + LANES]
        return dot(some_counts, ones)

    def rates():
        left = left_half(few)
        scale2[...] = 1.0 / (count2 + w2)
        rate = 1.0 / (fine_counts() + w1)
        rate1[...] = rate
        for p in range(n):
            low = rate[p * fine_dev : p * fine_dev + few]
            high = rate[p * fine_dev + few : (p + 1) * fine_dev]
            pull1[p * few : (p + 1) * few, :] = w1 * jnp.where(left, low, high)
        unpack(0)

    def bases():
        for t in range(1, tiles):
            unpack(t)
        sums1 = dot(h1f[...], got[...])
        for p in range(n):
            low = slice(p * fine_dev, p * fine_dev + few)
            high = slice(p * fine_dev + few, (p + 1) * fine_dev)
            place = slice(p * few, (p + 1) * few)
            for t in range(tiles):
                a = sums1[low, tile_of(t)] * rate1[low]
                b = sums1[high, tile_of(t)] * rate1[high]
                base1[2 * t, place, :] = halves(a, b, 0)
                base1[2 * t + 1, place, :] = halves(a, b, 1)

    def down(q):
        t, a = divmod(q, 2)
        from_owners(back_all.at[q : q + 1], back_recv.at[q])
        prior2 = back_all[q].astype(F32)
        prior2 = jnp.concatenate([prior2, prior2], axis=0).T
        means2 = (sums2[q] + w2 * prior2) * scale2[...]
        prior1 = dot(h1m[...], jnp.concatenate(pieces(means2, 2), axis=1))
        prior1 = prior1[:, 0:LANES] + prior1[:, LANES:]
        left = left_half(few)
        for p in range(n):
            low = prior1[p * fine_dev : p * fine_dev + few]
            high = prior1[p * fine_dev + few : (p + 1) * fine_dev]
            place = slice(p * few, (p + 1) * few)
            means1 = base1[q, place] + pull1[place] * jnp.where(left, low, high)
            fine_out[q, p] = means1.astype(BF)
        start(
            [
                remote(
                    fine_out.at[q, peer],
                    fine_in.at[q, me],
                    fine_send,
                    fine_recv.at[t],
                    {"clus": peer},
                )
                for k, peer in enumerate(peers)
            ]
        )
        if not a:
            mid_half[...] = means2
            return
        mid_own[:, tile_of(t)] = jnp.where(left_half(middle), mid_half[...], means2).astype(BF)
        start(
            [
                remote(
                    mid_own.at[span(peer, mid_share), tile_of(t)],
                    mid_ref.at[:, column(me, t)],
                    mid_send,
                    mid_recv,
                    {"clus": peer},
                )
                for peer in peers
            ]
        )
        copy = pltpu.make_async_copy(
            mid_own.at[span(me, mid_share), tile_of(t)], mid_ref.at[:, column(me, t)], local_sem.at[0]
        )
        copy.start()

    def rows_by_fine():
        fa_column = column_of(fa_row)
        for j in range(0, fine, LANES):
            h1r[:, j : j + LANES] = lanes_hot(fa_column, j)

    def coarse(t):
        from_owners(coarse_all.at[2 * t : 2 * t + 2], coarse_recv.at[t])
        block = jnp.concatenate([coarse_all[2 * t], coarse_all[2 * t + 1]], axis=0)
        coarse_own[:, tile_of(t)] = block.astype(F32).T.astype(BF)

        def place(peer):
            return coarse_own.at[span(side * n + peer, third_share), tile_of(t)]

        start(
            [
                remote(
                    place(peer), coarse_ref.at[:, column(me, t)], out_send, out_recv, {"clus": peer}
                )
                for peer in peers
            ]
        )
        copy = pltpu.make_async_copy(place(me), coarse_ref.at[:, column(me, t)], local_sem.at[1])
        copy.start()

    def fine_tile(t):
        for p in range(n):
            a, b = fine_out[2 * t, p], fine_out[2 * t + 1, p]
            fine_own[p * fine_dev : p * fine_dev + few, tile_of(t)] = halves(a, b, 0)
            fine_own[p * fine_dev + few : (p + 1) * fine_dev, tile_of(t)] = halves(a, b, 1)

    p1_row = jnp.concatenate([p1_all[i] for i in range(n)], axis=1) - dp * middle
    p1_column = column_of(p1_row)
    for j in range(0, middle, LANES):
        h1m[:, j : j + LANES] = lanes_hot(p1_column, j)
    sum_part(1)
    h1f[...] = rows_hot(fine, fa_row)
    rates()
    for q in range(2, chunks - 1):
        sum_part(q)
    when_near(third_counts)
    run_third(0)
    sum_part(chunks - 1)
    run_third(1)
    bases()
    run_third(2)
    down(0)
    for q in range(3, chunks):
        run_third(q)
    for q in range(1, chunks):
        down(q)
        if q == chunks - 2:
            coarse(0)
            fine_tile(0)
            rows_by_fine()
    if chunks == 2:
        rows_by_fine()
    coarse(tiles - 1)
    fine_tile(tiles - 1)
    fine_ref[:, span(me, share)] = fine_own[span(me, fine_dev), :]
    diff = got[...].astype(F32) - dot(h1r[...], fine_own[...])
    square = diff * diff
    folded = square[:, :LANES]
    for j in range(LANES, share, LANES):
        folded = folded + square[:, j : j + LANES]
    square = folded
    err_row = jnp.sum(square.T, axis=0, keepdims=True)
    parts = pieces(err_row, 3)
    line = lax.broadcasted_iota(jnp.int32, (16, n * count), 0)
    stack = jnp.where(line == 3, 1.0, 0.0)
    for i, part in enumerate(parts):
        stack = jnp.where(line == i, part.astype(F32), stack)
    by_fine = dot(stack.astype(BF), h1r[...])
    err_fine = by_fine[0:1] + by_fine[1:2] + by_fine[2:3]
    for i in range(n):
        err_own[i] = err_fine[:, i * fine_dev : (i + 1) * fine_dev]
        tally[i] = by_fine[3:4, i * fine_dev : (i + 1) * fine_dev]
    start(
        [
            remote(err_own.at[peer], err_all.at[me], err_send, err_recv, {"clus": peer})
            for peer in peers
        ]
    )
    err_all[me] = err_own[me]

    for t in range(tiles):
        landed(fine_in.at[2 * t : 2 * t + 2, 0 : n - 1], fine_recv.at[t])
        for k in range(1, n):
            peer = lax.rem(me + k, n)
            a, b = fine_in[2 * t, peer], fine_in[2 * t + 1, peer]
            fine_ref[0:few, column(peer, t)] = halves(a, b, 0)
            fine_ref[few:, column(peer, t)] = halves(a, b, 1)
    landed(err_all.at[0 : n - 1], err_recv)
    err = err_all[0]
    for i in range(1, n):
        err = err + err_all[i]
    spread_ref[...] = err / (width * (tally[me] + 1.0))
    landed(mid_ref.at[:, 0:share], local_sem.at[0])
    landed(coarse_ref.at[:, 0:share], local_sem.at[1])
    landed(mid_ref.at[:, 0 : (n - 1) * share], mid_recv)
    landed(coarse_ref.at[:, 0 : (n - 1) * share], out_recv)
    landed(fa_all.at[0 : n - 1], id_send.at[0])
    landed(p1_all.at[0 : n - 1], id_send.at[1])
    landed(row_out.at[:, 0 : n - 1], row_send)
    landed(fine_out.at[:, 0 : n - 1], fine_send)
    landed(mid_own.at[0 : (n - 1) * mid_share], mid_send)
    landed(coarse_own.at[0 : (n - 1) * third_share], out_send)
    landed(err_own.at[0 : n - 1], err_send)

    @when_outer
    def _():
        landed(p2_all.at[0:size], p2_send)
        landed(cnt_all.at[0:size], cnt_send)
        landed(part_own, part_send)

    @when_near
    def _():
        landed(p2_all.at[0 : size - 1], p2_send)
        landed(cnt_all.at[0 : size - 1], cnt_send)
        landed(part_own.at[:, 0 : (size - 1) * thin], part_send)
        landed(back_own.at[:, :, 0 : (m - 1) * middle], back_send.at[0])
        landed(back_own.at[:, :, 0 : (m - 1) * window], back_send.at[1])


def land(count, *refs):
    sem = refs[-1]
    pairs = zip(refs[:count], refs[count : 2 * count])
    copies = [pltpu.make_async_copy(a, b, sem.at[i]) for i, (a, b) in enumerate(pairs)]
    for copy in copies:
        copy.start()
    for copy in copies:
        copy.wait()


def settle(*arrays):
    count = len(arrays)
    return pl.pallas_call(
        functools.partial(land, count),
        out_shape=tuple(jax.ShapeDtypeStruct(a.shape, a.dtype) for a in arrays),
        in_specs=[pl.BlockSpec(memory_space=pltpu.VMEM)] * count,
        out_specs=tuple([pl.BlockSpec(memory_space=pl.ANY)] * count),
        scratch_shapes=[pltpu.SemaphoreType.DMA((count,))],
        compiler_params=pltpu.CompilerParams(vmem_limit_bytes=4 << 20),
        name="settle",
    )(*arrays)


def fused(rows, fine_assign, parent1, parent2, parent3, shrink):
    n = lax.axis_size("clus")
    m = lax.axis_size("dp")
    count, width = rows.shape
    fine_dev = parent1.shape[0]
    middle = parent2.shape[0]
    third = parent3.shape[0]
    share = width // n
    tiles = share // LANES
    chunks = 2 * tiles
    window = third // (m // 2)
    fine = n * fine_dev
    total_rows = n * count
    vmem = pl.BlockSpec(memory_space=pltpu.VMEM)
    hbm = pl.BlockSpec(memory_space=pltpu.HBM)
    dma = pltpu.SemaphoreType.DMA

    def stay(x):
        return pltpu.with_memory_space_constraint(x, pltpu.HBM)

    fine_out, mid_out, coarse_out, spread = pl.pallas_call(
        functools.partial(sweep, n, m),
        out_shape=(
            jax.ShapeDtypeStruct((fine_dev, width), BF),
            jax.ShapeDtypeStruct((middle // n, width), BF),
            jax.ShapeDtypeStruct((third // (n * m), width), BF),
            jax.ShapeDtypeStruct((1, fine_dev), F32),
        ),
        in_specs=[hbm] * 6,
        out_specs=[vmem] * 4,
        scratch_shapes=[
            pltpu.VMEM((n, 1, count), jnp.int32),
            pltpu.VMEM((n, 1, fine_dev), jnp.int32),
            pltpu.VMEM((m, 1, middle), jnp.int32),
            pltpu.VMEM((1, third), jnp.int32),
            pltpu.SMEM((4,), F32),
            pltpu.VMEM((count, width), BF),
            pltpu.VMEM((chunks, n, count // 2, LANES), BF),
            pltpu.VMEM((chunks, total_rows // 2, LANES), BF),
            pltpu.VMEM((total_rows, share), BF),
            pltpu.VMEM((fine, total_rows), BF),
            pltpu.VMEM((middle, total_rows), BF),
            pltpu.VMEM((total_rows, fine), BF),
            pltpu.VMEM((fine, middle), BF),
            pltpu.VMEM((third, m * middle), BF),
            pltpu.VMEM((m * middle, third), BF),
            pltpu.VMEM((chunks, middle, LANES), F32),
            pltpu.VMEM((chunks, fine // 2, LANES), F32),
            pltpu.VMEM((fine // 2, LANES), F32),
            pltpu.VMEM((middle, LANES), F32),
            pltpu.VMEM((fine, LANES), F32),
            pltpu.VMEM((chunks, HALF, middle), BF),
            pltpu.VMEM((chunks, m, HALF // 4, middle), BF),
            pltpu.VMEM((1, middle), F32),
            pltpu.VMEM((m, 1, middle), F32),
            pltpu.VMEM((1, third), F32),
            pltpu.VMEM((1, LANES), F32),
            pltpu.VMEM((chunks, HALF // 4, third), BF),
            pltpu.VMEM((chunks, HALF // 4, m * middle), BF),
            pltpu.VMEM((chunks, HALF, middle), BF),
            pltpu.VMEM((chunks, HALF, window), BF),
            pltpu.VMEM((middle, LANES), F32),
            pltpu.VMEM((chunks, n, fine_dev // 2, LANES), BF),
            pltpu.VMEM((chunks, n, fine_dev // 2, LANES), BF),
            pltpu.VMEM((fine, share), BF),
            pltpu.VMEM((middle, share), BF),
            pltpu.VMEM((window, share), BF),
            pltpu.VMEM((n, 1, fine_dev), F32),
            pltpu.VMEM((n, 1, fine_dev), F32),
            pltpu.VMEM((n, 1, fine_dev), F32),
            dma((6,)),
            dma((2,)),
            dma((2,)),
            dma,
            dma,
            dma,
            dma((chunks,)),
            dma,
            dma((chunks,)),
            dma,
            dma,
            dma((2,)),
            dma((chunks,)),
            dma((tiles,)),
            dma,
            dma((tiles,)),
            dma,
            dma,
            dma,
            dma,
            dma,
            dma,
            dma((2,)),
        ],
        compiler_params=pltpu.CompilerParams(
            collective_id=0, has_side_effects=True, vmem_limit_bytes=40 << 20
        ),
        name="sweep",
    )(
        stay(fine_assign.reshape(1, count)),
        stay(parent1.reshape(1, fine_dev)),
        stay(parent2.reshape(1, middle)),
        stay(parent3.reshape(1, third)),
        stay(shrink),
        stay(rows),
    )
    fine_out, mid_out, coarse_out, spread = settle(fine_out, mid_out, coarse_out, spread)
    return fine_out, mid_out, coarse_out, spread.reshape(fine_dev)


def fits(rows, fine_assign, parent1, parent2, parent3):
    n = lax.axis_size("clus")
    m = lax.axis_size("dp")
    return (
        rows.shape[1] == 2 * n * LANES
        and m % 4 == 0
        and rows.shape[0] % (2 * LANES) == 0
        and parent1.shape[0] % (2 * LANES) == 0
        and parent2.shape[0] % LANES == 0
        and parent2.shape[0] <= 256
        and parent2.shape[0] % (n * 16) == 0
        and parent3.shape[0] % (m // 2 * LANES) == 0
        and parent3.shape[0] // (m // 2) <= parent2.shape[0]
        and parent3.shape[0] % (n * m * 16) == 0
    )


def step(rows, fine_assign, parent1, parent2, parent3, shrink):
    form = fused if fits(rows, fine_assign, parent1, parent2, parent3) else local
    return form(rows, fine_assign, parent1, parent2, parent3, shrink)


def solution(mesh):
    placed = (P(("dp", "clus"), None), P(("dp", "clus")), P(("dp", "clus")), P("dp"), P(), P())
    return jax.shard_map(
        step,
        mesh=mesh,
        in_specs=placed,
        out_specs=(
            P(("dp", "clus"), None),
            P(("dp", "clus"), None),
            P(("dp", "clus"), None),
            P(("dp", "clus")),
        ),
        check_vma=False,
    )
```

```python
import functools

import jax
import jax.numpy as jnp
from jax import lax
from jax.experimental import pallas as pl
from jax.experimental.pallas import tpu as pltpu
from jax.sharding import PartitionSpec as P

K4 = 64


HIGH = lax.Precision.HIGHEST


def shrunk(sums, counts, prior, weight):
    return (sums + weight * prior) / (counts + weight)[:, None]


def local(rows, fine_assign, parent1, parent2, parent3, shrink):
    groups = lax.axis_size("clus")
    dp_count = lax.axis_size("dp")
    devices = groups * dp_count
    clus_index = lax.axis_index("clus")
    dp_index = lax.axis_index("dp")
    count = rows.shape[0]
    width = rows.shape[1]
    fine_dev = parent1.shape[0]
    middle_dp = parent2.shape[0]
    third = parent3.shape[0]
    slots = 2 * count // groups
    total = count * devices
    weight_top = shrink[0] * (total / K4)
    weight_third = shrink[1] * (total / third)
    weight_middle = shrink[2] * (total / (middle_dp * dp_count))
    weight_fine = shrink[3] * (total / (fine_dev * devices))
    local_ids = fine_assign - dp_index * groups * fine_dev
    target = local_ids // fine_dev
    within = local_ids - target * fine_dev
    target_hot = (target[:, None] == jnp.arange(groups)[None, :]).astype(jnp.bfloat16)
    earlier = (jnp.arange(count)[:, None] > jnp.arange(count)[None, :]).astype(jnp.bfloat16)
    before = jnp.dot(earlier, target_hot, preferred_element_type=jnp.float32)
    rank = jnp.sum(before * target_hot.astype(jnp.float32), axis=1).astype(jnp.int32)
    slot_of = target * slots + rank
    source = (
        jnp.full((groups * slots,), count, jnp.int32)
        .at[slot_of]
        .set(jnp.arange(count, dtype=jnp.int32))
    )
    padded = jnp.concatenate([rows, jnp.zeros((1, width), jnp.bfloat16)], axis=0)
    send_rows = padded[source].reshape(groups, slots, width)
    send_ids = jnp.concatenate([within, jnp.full((1,), -1, jnp.int32)])[source].reshape(
        groups, slots
    )
    got_rows, got_ids = (
        lax.all_to_all(send_rows, "clus", split_axis=0, concat_axis=0, tiled=True),
        lax.all_to_all(send_ids, "clus", split_axis=0, concat_axis=0, tiled=True),
    )
    got_rows = got_rows.reshape(groups * slots, width)
    got_ids = got_ids.reshape(groups * slots)
    member = (got_ids[:, None] == jnp.arange(fine_dev)[None, :]).astype(jnp.bfloat16)
    contract = (((0,), (0,)), ((), ()))
    fine_sums = lax.dot_general(member, got_rows, contract, preferred_element_type=jnp.float32)
    fine_counts = jnp.sum(member.astype(jnp.float32), axis=0)
    middle_local = parent1 - dp_index * middle_dp
    child_hot = (jnp.arange(middle_dp)[:, None] == middle_local[None, :]).astype(jnp.float32)
    middle_part = jnp.dot(child_hot, fine_sums, precision=HIGH)
    middle_tally = jnp.dot(child_hot, fine_counts, precision=HIGH)
    share = middle_dp // groups
    offset = clus_index * share
    middle_sums, middle_counts = (
        lax.psum_scatter(middle_part, "clus", scatter_dimension=0, tiled=True),
        lax.psum_scatter(middle_tally, "clus", scatter_dimension=0, tiled=True),
    )
    own_parent2 = lax.dynamic_slice_in_dim(parent2, offset, share, 0)
    third_share = third // devices
    third_start = (dp_index * groups + clus_index) * third_share
    third_hot = (jnp.arange(third)[:, None] == own_parent2[None, :]).astype(jnp.float32)
    third_part = jnp.dot(third_hot, middle_sums, precision=HIGH)
    third_tally = jnp.dot(third_hot, middle_counts, precision=HIGH)
    third_sums, third_counts = lax.psum((third_part, third_tally), ("dp", "clus"))
    top_hot = (jnp.arange(K4)[:, None] == parent3[None, :]).astype(jnp.float32)
    top_sums = jnp.dot(top_hot, third_sums, precision=HIGH)
    top_counts = jnp.dot(top_hot, third_counts, precision=HIGH)
    center = jnp.sum(top_sums, axis=0) / total
    top_means = shrunk(top_sums, top_counts, center[None, :], weight_top)
    third_means = shrunk(
        third_sums, third_counts, jnp.dot(top_hot.T, top_means, precision=HIGH), weight_third
    )
    third_out = lax.dynamic_slice_in_dim(third_means, third_start, third_share, 0)
    parent_hot = (own_parent2[:, None] == jnp.arange(third)[None, :]).astype(jnp.float32)
    middle_out = shrunk(
        middle_sums, middle_counts, jnp.dot(parent_hot, third_means, precision=HIGH), weight_middle
    )
    middle_means = lax.all_gather(middle_out, "clus", axis=0, tiled=True)
    fine_means = shrunk(
        fine_sums, fine_counts, jnp.dot(child_hot.T, middle_means, precision=HIGH), weight_fine
    )
    fine_out = fine_means.astype(jnp.bfloat16)
    back = jnp.dot(member, fine_out, preferred_element_type=jnp.float32)
    diff = got_rows.astype(jnp.float32) - back
    row_error = jnp.sum(diff * diff, axis=1)
    spread = jnp.sum(member.astype(jnp.float32) * row_error[:, None], axis=0) / (
        width * (fine_counts + 1.0)
    )
    return (fine_out, middle_out.astype(jnp.bfloat16), third_out.astype(jnp.bfloat16), spread)


LANES = 128
HALF = LANES // 2
BF = jnp.bfloat16
F32 = jnp.float32
MESH = pl.DeviceIdType.MESH


def rows_hot(size, ids):
    shape = (size, ids.shape[1])
    lines = lax.broadcasted_iota(jnp.int16, shape, 0)
    same = lines == jnp.broadcast_to(ids.astype(jnp.int16), shape)
    return jnp.where(same, jnp.ones(shape, BF), jnp.zeros(shape, BF))


def column_of(ids):
    column = jnp.broadcast_to(ids.astype(F32), (LANES, ids.shape[1])).T
    return column.astype(jnp.int32).astype(jnp.int16)


def lanes_hot(column, start):
    shape = column.shape
    same = column == lax.broadcasted_iota(jnp.int16, shape, 1) + jnp.int16(start)
    return jnp.where(same, jnp.ones(shape, BF), jnp.zeros(shape, BF))


def dot(a, b):
    return jnp.dot(a, b, preferred_element_type=F32)


def pieces(x, count):
    out = []
    for _ in range(count):
        part = x.astype(BF)
        out.append(part)
        x = x - part.astype(F32)
    return out


def dot_left(x, hot, count=3):
    return sum(dot(part, hot) for part in pieces(x, count))


def halves(a, b, part):
    lane = slice(part * HALF, (part + 1) * HALF)
    return jnp.concatenate([a[:, lane], b[:, lane]], axis=1)


def dot_stack(x, hot):
    both = dot(jnp.concatenate(pieces(x, 2), axis=0), hot)
    return both[: x.shape[0]] + both[x.shape[0] :]


def sweep(
    n,
    m,
    fa_hbm,
    p1_hbm,
    p2_hbm,
    p3_hbm,
    shrink_hbm,
    rows_ref,
    fine_ref,
    mid_ref,
    coarse_ref,
    spread_ref,
    fa_all,
    p1_all,
    p2_all,
    p3_ref,
    shrink_ref,
    rows_own,
    row_out,
    row_in,
    got,
    h1f,
    h2f,
    h1r,
    h1m,
    ht,
    hn,
    sums2,
    base1,
    pull1,
    scale2,
    rate1,
    part_own,
    part_all,
    cnt_own,
    cnt_all,
    rate3,
    rate4,
    means3,
    back_own,
    back_all,
    coarse_all,
    mid_half,
    fine_out,
    fine_in,
    fine_own,
    mid_own,
    coarse_own,
    err_own,
    err_all,
    tally,
    in_sem,
    id_send,
    id_recv,
    p2_send,
    p2_recv,
    row_send,
    row_recv,
    part_send,
    part_recv,
    cnt_send,
    cnt_recv,
    back_send,
    back_recv,
    coarse_recv,
    fine_send,
    fine_recv,
    mid_send,
    mid_recv,
    out_send,
    out_recv,
    err_send,
    err_recv,
    local_sem,
):
    me = lax.axis_index("clus")
    dp = lax.axis_index("dp")
    count, width = rows_ref.shape
    share = width // n
    tiles = share // LANES
    chunks = 2 * tiles
    fine_dev = p1_hbm.shape[1]
    middle = p2_hbm.shape[1]
    third = p3_hbm.shape[1]
    devices = n * m
    total = count * devices
    fine = n * fine_dev
    some = count // 2
    few = fine_dev // 2
    packed = n * some
    center_dp = m // 2 // 2 * 2
    pairs = m // 2
    pair = dp // 2
    side = lax.rem(dp, 2)
    near = (center_dp // 2 - 1, center_dp // 2)
    size = 4
    thin = HALF // size
    window = third // pairs
    mid_share = middle // n
    third_share = third // devices

    def span(index, size):
        return pl.ds(pl.multiple_of(index * size, size), size)

    def tile_of(t):
        return slice(t * LANES, (t + 1) * LANES)

    def column(index, t):
        return pl.ds(pl.multiple_of(index * share + t * LANES, LANES), LANES)

    def remote(src, dst, send, recv, device):
        return pltpu.make_async_remote_copy(
            src_ref=src,
            dst_ref=dst,
            send_sem=send,
            recv_sem=recv,
            device_id=device,
            device_id_type=MESH,
        )

    if n == 4:
        peers = [n - 1 - me, jnp.where(side == 0, lax.rem(me + 2, n), me + 1 - 2 * lax.rem(me, 2)), jnp.where(side == 0, me + 1 - 2 * lax.rem(me, 2), lax.rem(me + 2, n))]
    else:
        peers = [lax.rem(me + k, n) for k in range(1, n)]

    def start(copies):
        for copy in copies:
            copy.start()

    def landed(ref, sem):
        pltpu.make_async_copy(ref, ref, sem).wait()

    low_half = pair < pairs // 2

    close = jnp.where(low_half, near[0], near[1])
    away = jnp.where(low_half, near[1], near[0])
    block = jnp.where(low_half, 2, 0)
    owners = (
        (away * 2, block),
        (away * 2 + 1, block + 1),
        (close * 2 + 1 - side, 2 - block + 1 - side),
        (close * 2 + side, 2 - block + side),
    )
    slot = owners[3][1]
    in_near = pair == close
    outer = [2 * chip + core for chip in range(pairs) if chip not in near for core in range(2)]

    def when_near(run):
        pl.when(in_near)(run)

    def when_outer(run):
        pl.when(jnp.logical_not(in_near))(run)

    def to_owners(do):
        for k in range(size - 1):
            do(k)
        when_outer(lambda: do(size - 1))

    if pairs == 4:
        inward = jnp.where(low_half, pair + 1, pair - 1)
        last = jnp.where(low_half, 3, 0)
        chips = [inward, 6 - pair - inward - last, last]
    else:
        chips = [lax.rem(pair + k, pairs) for k in range(1, pairs)]
    others = [chip * 2 + core for chip in reversed(chips) for core in range(2)]
    others.append(pair * 2 + 1 - side)

    barrier = pltpu.get_barrier_semaphore()
    for peer in peers:
        pl.semaphore_signal(barrier, inc=1, device_id={"clus": peer}, device_id_type=MESH)
    def greet(device):
        pl.semaphore_signal(barrier, inc=1, device_id={"dp": device}, device_id_type=MESH)

    to_owners(lambda k: greet(owners[k][0]))

    @when_near
    def _():
        for device in outer:
            greet(device)

    fetch = [
        pltpu.make_async_copy(src, dst, in_sem.at[i])
        for i, (src, dst) in enumerate(
            (
                (fa_hbm, fa_all.at[me]),
                (p1_hbm, p1_all.at[me]),
                (p2_hbm, p2_all.at[dp]),
                (rows_ref, rows_own),
                (p3_hbm, p3_ref),
                (shrink_hbm, shrink_ref),
            )
        )
    ]
    for copy in fetch:
        copy.start()

    def pack(q):
        t, a = divmod(q, 2)
        for p in range(n):
            lane = slice(p * share + t * LANES, p * share + (t + 1) * LANES)
            row_out[q, p] = halves(rows_own[0:some, lane], rows_own[some:count, lane], a)

    fetch[3].wait()
    for q in range(1):
        pack(q)
    pl.semaphore_wait(barrier, n - 1 + jnp.where(in_near, m - 1, size))
    for copy in fetch[:3]:
        copy.wait()

    for peer in peers:
        for which, ids in enumerate((fa_all, p1_all)):
            own = ids.at[me]
            start([remote(own, own, id_send.at[which], id_recv.at[which], {"clus": peer})])

    def p2_copy(k):
        own = p2_all.at[dp]
        return remote(own, own, p2_send, p2_recv, {"dp": owners[k][0]})

    to_owners(lambda k: p2_copy(k).start())
    for q in range(chunks):
        if q >= 1:
            pack(q)
        start(
            [
                remote(
                    row_out.at[q, peer],
                    row_in.at[q, span(me, some), :],
                    row_send,
                    row_recv.at[q],
                    {"clus": peer},
                )
                for peer in peers
            ]
        )
    for q in range(chunks):
        row_in[q, span(me, some), :] = row_out[q, me]

    for copy in fetch[4:]:
        copy.wait()
    w4 = shrink_ref[0] * (total / K4)
    w3 = shrink_ref[1] * (total / third)
    w2 = shrink_ref[2] * (total / (middle * m))
    w1 = shrink_ref[3] * (total / (fine_dev * devices))
    p3_row = p3_ref[...]
    upper = lax.broadcasted_iota(jnp.int32, (third, LANES), 1) >= K4
    h4 = jnp.where(upper, 1.0, lanes_hot(column_of(p3_row), 0).astype(F32)).astype(BF)
    h4f = rows_hot(LANES, p3_row)
    ones = jnp.ones((LANES, LANES), BF)

    def left_half(size):
        return lax.broadcasted_iota(jnp.int32, (size, LANES), 1) < HALF

    def parents_of(i):
        row = p2_all[i]
        ht[:, span(i, middle)] = rows_hot(third, row)
        p2_column = column_of(row)
        for j in range(0, third, LANES):
            hn[span(i, middle), j : j + LANES] = lanes_hot(p2_column, j)

    @when_near
    def _():
        parents_of(dp)

    landed(fa_all.at[0 : n - 1], id_recv.at[0])
    landed(p1_all.at[0 : n - 1], id_recv.at[1])
    ids = [fa_all[i] for i in range(n)]
    ids = [x[:, 0:some] for x in ids] + [x[:, some:count] for x in ids]
    fa_row = jnp.concatenate(ids, axis=1) - dp * fine
    table = [
        p1_all[i][:, j : j + LANES] for i in range(n) for j in range(0, fine_dev, LANES)
    ]
    table = (jnp.concatenate(table, axis=0) - dp * middle).astype(F32).astype(BF)
    line = fa_row // LANES
    picked = dot(table, rows_hot(LANES, fa_row - line * LANES))
    lines = lax.broadcasted_iota(jnp.int32, picked.shape, 0)
    mid_row = jnp.sum(jnp.where(lines == line, picked, 0.0), axis=0, keepdims=True)
    h2f[...] = rows_hot(middle, mid_row.astype(jnp.int32))

    def part_copy(q, k):
        device, o = owners[k]
        return remote(
            part_own.at[q, span(o, thin), :],
            part_all.at[q, dp],
            part_send,
            part_recv.at[q],
            {"dp": device},
        )

    def cnt_copy(k):
        place = {"dp": owners[k][0]}
        return remote(cnt_own, cnt_all.at[dp], cnt_send, cnt_recv, place)

    def sum_part(q):
        landed(row_in.at[q, 0 : (n - 1) * some], row_recv.at[q])
        block = row_in[q]
        both = jnp.where(
            left_half(middle), dot(h2f[:, 0:packed], block), dot(h2f[:, packed:], block)
        )
        turned = both.T
        part_own[q] = (turned[0:HALF] + turned[HALF:]).astype(BF)
        to_owners(lambda k: part_copy(q, k).start())

        @when_near
        def _():
            part_all[q, dp] = part_own[q, span(slot, thin), :]

        sums2[q] = both + pltpu.roll(both, HALF, 1)

    count2 = h2f[:, 0:LANES]
    for j in range(LANES, n * count, LANES):
        count2 = count2 + h2f[:, j : j + LANES]
    count2 = dot(count2, ones)
    cnt_own[...] = count2.T[0:1]
    to_owners(lambda k: cnt_copy(k).start())
    cnt_all[dp] = cnt_own[...]
    sum_part(0)
    @when_near
    def _():
        landed(p2_all.at[0 : m - 1], p2_recv)
        for i in others:
            parents_of(i)


    def back_copy(q, k):
        peer = others[k]
        return remote(
            back_own.at[q, :, span(peer, middle)],
            back_all.at[q, span(slot, thin), :],
            back_send.at[0],
            back_recv.at[q],
            {"dp": peer},
        )

    def coarse_copy(q, k):
        peer = others[k]
        return remote(
            means3.at[q, :, span(peer // 2, window)],
            coarse_all.at[q, span(slot, thin), :],
            back_send.at[1],
            coarse_recv.at[q // 2],
            {"dp": peer},
        )

    def from_owners(ref, sem):
        when_near(lambda: landed(ref.at[:, 0 : (size - 1) * thin], sem))
        when_outer(lambda: landed(ref, sem))

    def third_counts():
        landed(cnt_all.at[0 : m - 1], cnt_recv)
        lines = jnp.concatenate([cnt_all[i] for i in range(m)], axis=1)
        row = lax.broadcasted_iota(jnp.int32, (16, m * middle), 0)
        stack = jnp.zeros((16, m * middle), F32)
        for i, part in enumerate(pieces(lines, 3)):
            stack = jnp.where(row == i, part.astype(F32), stack)
        cnt3 = dot(stack.astype(BF), hn[...])
        cnt3 = cnt3[0:1] + cnt3[1:2] + cnt3[2:3]
        rate3[...] = 1.0 / (cnt3 + w3)
        cnt4 = dot_stack(jnp.broadcast_to(cnt3, (16, third)), h4)[0:1]
        rate4[...] = 1.0 / (cnt4 + w4)

    def third_level(q):
        landed(part_all.at[q, 0 : m - 1], part_recv.at[q])
        sums3 = dot(jnp.concatenate([part_all[q, i] for i in range(m)], axis=1), hn[...])
        sums4 = dot_stack(sums3, h4)
        center = pltpu.roll(sums4, K4, 1) / total
        means4 = (sums4 + w4 * center) * rate4[...]
        block = ((sums3 + w3 * dot_stack(means4, h4f)) * rate3[...]).astype(BF)
        means3[q] = block
        back_own[q] = dot(block, ht[...]).astype(BF)
        for k in range(m - 1):
            back_copy(q, k).start()
        for k in range(m - 1):
            coarse_copy(q, k).start()
        back_all[q, span(slot, thin), :] = back_own[q, :, span(dp, middle)]
        coarse_all[q, span(slot, thin), :] = means3[q, :, span(dp // 2, window)]

    def run_third(q):
        when_near(lambda: third_level(q))

    def unpack(t):
        a, b = row_in[2 * t], row_in[2 * t + 1]
        got[0:packed, tile_of(t)] = halves(a, b, 0)
        got[packed:, tile_of(t)] = halves(a, b, 1)

    def fine_counts():
        some_counts = h1f[:, 0:LANES]
        for j in range(LANES, n * count, LANES):
            some_counts = some_counts + h1f[:, j : j + LANES]
        return dot(some_counts, ones)

    def rates():
        left = left_half(few)
        scale2[...] = 1.0 / (count2 + w2)
        rate = 1.0 / (fine_counts() + w1)
        rate1[...] = rate
        for p in range(n):
            low = rate[p * fine_dev : p * fine_dev + few]
            high = rate[p * fine_dev + few : (p + 1) * fine_dev]
            pull1[p * few : (p + 1) * few, :] = w1 * jnp.where(left, low, high)
        unpack(0)

    def bases():
        for t in range(1, tiles):
            unpack(t)
        sums1 = dot(h1f[...], got[...])
        for p in range(n):
            low = slice(p * fine_dev, p * fine_dev + few)
            high = slice(p * fine_dev + few, (p + 1) * fine_dev)
            place = slice(p * few, (p + 1) * few)
            for t in range(tiles):
                a = sums1[low, tile_of(t)] * rate1[low]
                b = sums1[high, tile_of(t)] * rate1[high]
                base1[2 * t, place, :] = halves(a, b, 0)
                base1[2 * t + 1, place, :] = halves(a, b, 1)

    def down(q):
        t, a = divmod(q, 2)
        from_owners(back_all.at[q : q + 1], back_recv.at[q])
        prior2 = back_all[q].astype(F32)
        prior2 = jnp.concatenate([prior2, prior2], axis=0).T
        means2 = (sums2[q] + w2 * prior2) * scale2[...]
        prior1 = dot(h1m[...], jnp.concatenate(pieces(means2, 2), axis=1))
        prior1 = prior1[:, 0:LANES] + prior1[:, LANES:]
        left = left_half(few)
        for p in range(n):
            low = prior1[p * fine_dev : p * fine_dev + few]
            high = prior1[p * fine_dev + few : (p + 1) * fine_dev]
            place = slice(p * few, (p + 1) * few)
            means1 = base1[q, place] + pull1[place] * jnp.where(left, low, high)
            fine_out[q, p] = means1.astype(BF)
        start(
            [
                remote(
                    fine_out.at[q, peer],
                    fine_in.at[q, me],
                    fine_send,
                    fine_recv.at[t],
                    {"clus": peer},
                )
                for k, peer in enumerate(peers)
            ]
        )
        if not a:
            mid_half[...] = means2
            return
        mid_own[:, tile_of(t)] = jnp.where(left_half(middle), mid_half[...], means2).astype(BF)
        start(
            [
                remote(
                    mid_own.at[span(peer, mid_share), tile_of(t)],
                    mid_ref.at[:, column(me, t)],
                    mid_send,
                    mid_recv,
                    {"clus": peer},
                )
                for peer in peers
            ]
        )
        copy = pltpu.make_async_copy(
            mid_own.at[span(me, mid_share), tile_of(t)], mid_ref.at[:, column(me, t)], local_sem.at[0]
        )
        copy.start()

    def rows_by_fine():
        fa_column = column_of(fa_row)
        for j in range(0, fine, LANES):
            h1r[:, j : j + LANES] = lanes_hot(fa_column, j)

    def coarse(t):
        from_owners(coarse_all.at[2 * t : 2 * t + 2], coarse_recv.at[t])
        block = jnp.concatenate([coarse_all[2 * t], coarse_all[2 * t + 1]], axis=0)
        coarse_own[:, tile_of(t)] = block.astype(F32).T.astype(BF)

        def place(peer):
            return coarse_own.at[span(side * n + peer, third_share), tile_of(t)]

        start(
            [
                remote(
                    place(peer), coarse_ref.at[:, column(me, t)], out_send, out_recv, {"clus": peer}
                )
                for peer in peers
            ]
        )
        copy = pltpu.make_async_copy(place(me), coarse_ref.at[:, column(me, t)], local_sem.at[1])
        copy.start()

    def fine_tile(t):
        for p in range(n):
            a, b = fine_out[2 * t, p], fine_out[2 * t + 1, p]
            fine_own[p * fine_dev : p * fine_dev + few, tile_of(t)] = halves(a, b, 0)
            fine_own[p * fine_dev + few : (p + 1) * fine_dev, tile_of(t)] = halves(a, b, 1)

    p1_row = jnp.concatenate([p1_all[i] for i in range(n)], axis=1) - dp * middle
    p1_column = column_of(p1_row)
    for j in range(0, middle, LANES):
        h1m[:, j : j + LANES] = lanes_hot(p1_column, j)
    sum_part(1)
    h1f[...] = rows_hot(fine, fa_row)
    rates()
    for q in range(2, chunks - 1):
        sum_part(q)
    when_near(third_counts)
    run_third(0)
    sum_part(chunks - 1)
    run_third(1)
    bases()
    run_third(2)
    down(0)
    for q in range(3, chunks):
        run_third(q)
    for q in range(1, chunks):
        down(q)
        if q == chunks - 2:
            coarse(0)
            fine_tile(0)
            rows_by_fine()
    if chunks == 2:
        rows_by_fine()
    coarse(tiles - 1)
    fine_tile(tiles - 1)
    fine_ref[:, span(me, share)] = fine_own[span(me, fine_dev), :]
    diff = got[...].astype(F32) - dot(h1r[...], fine_own[...])
    square = diff * diff
    folded = square[:, :LANES]
    for j in range(LANES, share, LANES):
        folded = folded + square[:, j : j + LANES]
    square = folded
    err_row = jnp.sum(square.T, axis=0, keepdims=True)
    parts = pieces(err_row, 3)
    line = lax.broadcasted_iota(jnp.int32, (16, n * count), 0)
    stack = jnp.where(line == 3, 1.0, 0.0)
    for i, part in enumerate(parts):
        stack = jnp.where(line == i, part.astype(F32), stack)
    by_fine = dot(stack.astype(BF), h1r[...])
    err_fine = by_fine[0:1] + by_fine[1:2] + by_fine[2:3]
    for i in range(n):
        err_own[i] = err_fine[:, i * fine_dev : (i + 1) * fine_dev]
        tally[i] = by_fine[3:4, i * fine_dev : (i + 1) * fine_dev]
    start(
        [
            remote(err_own.at[peer], err_all.at[me], err_send, err_recv, {"clus": peer})
            for peer in peers
        ]
    )
    err_all[me] = err_own[me]

    for t in range(tiles):
        landed(fine_in.at[2 * t : 2 * t + 2, 0 : n - 1], fine_recv.at[t])
        for k in range(1, n):
            peer = lax.rem(me + k, n)
            a, b = fine_in[2 * t, peer], fine_in[2 * t + 1, peer]
            fine_ref[0:few, column(peer, t)] = halves(a, b, 0)
            fine_ref[few:, column(peer, t)] = halves(a, b, 1)
    landed(err_all.at[0 : n - 1], err_recv)
    err = err_all[0]
    for i in range(1, n):
        err = err + err_all[i]
    spread_ref[...] = err / (width * (tally[me] + 1.0))
    landed(mid_ref.at[:, 0:share], local_sem.at[0])
    landed(coarse_ref.at[:, 0:share], local_sem.at[1])
    landed(mid_ref.at[:, 0 : (n - 1) * share], mid_recv)
    landed(coarse_ref.at[:, 0 : (n - 1) * share], out_recv)
    landed(fa_all.at[0 : n - 1], id_send.at[0])
    landed(p1_all.at[0 : n - 1], id_send.at[1])
    landed(row_out.at[:, 0 : n - 1], row_send)
    landed(fine_out.at[:, 0 : n - 1], fine_send)
    landed(mid_own.at[0 : (n - 1) * mid_share], mid_send)
    landed(coarse_own.at[0 : (n - 1) * third_share], out_send)
    landed(err_own.at[0 : n - 1], err_send)

    @when_outer
    def _():
        landed(p2_all.at[0:size], p2_send)
        landed(cnt_all.at[0:size], cnt_send)
        landed(part_own, part_send)

    @when_near
    def _():
        landed(p2_all.at[0 : size - 1], p2_send)
        landed(cnt_all.at[0 : size - 1], cnt_send)
        landed(part_own.at[:, 0 : (size - 1) * thin], part_send)
        landed(back_own.at[:, :, 0 : (m - 1) * middle], back_send.at[0])
        landed(back_own.at[:, :, 0 : (m - 1) * window], back_send.at[1])


def land(count, *refs):
    sem = refs[-1]
    pairs = zip(refs[:count], refs[count : 2 * count])
    copies = [pltpu.make_async_copy(a, b, sem.at[i]) for i, (a, b) in enumerate(pairs)]
    for copy in copies:
        copy.start()
    for copy in copies:
        copy.wait()


def settle(*arrays):
    count = len(arrays)
    return pl.pallas_call(
        functools.partial(land, count),
        out_shape=tuple(jax.ShapeDtypeStruct(a.shape, a.dtype) for a in arrays),
        in_specs=[pl.BlockSpec(memory_space=pltpu.VMEM)] * count,
        out_specs=tuple([pl.BlockSpec(memory_space=pl.ANY)] * count),
        scratch_shapes=[pltpu.SemaphoreType.DMA((count,))],
        compiler_params=pltpu.CompilerParams(vmem_limit_bytes=4 << 20),
        name="settle",
    )(*arrays)


def fused(rows, fine_assign, parent1, parent2, parent3, shrink):
    n = lax.axis_size("clus")
    m = lax.axis_size("dp")
    count, width = rows.shape
    fine_dev = parent1.shape[0]
    middle = parent2.shape[0]
    third = parent3.shape[0]
    share = width // n
    tiles = share // LANES
    chunks = 2 * tiles
    window = third // (m // 2)
    fine = n * fine_dev
    total_rows = n * count
    vmem = pl.BlockSpec(memory_space=pltpu.VMEM)
    hbm = pl.BlockSpec(memory_space=pltpu.HBM)
    dma = pltpu.SemaphoreType.DMA

    def stay(x):
        return pltpu.with_memory_space_constraint(x, pltpu.HBM)

    fine_out, mid_out, coarse_out, spread = pl.pallas_call(
        functools.partial(sweep, n, m),
        out_shape=(
            jax.ShapeDtypeStruct((fine_dev, width), BF),
            jax.ShapeDtypeStruct((middle // n, width), BF),
            jax.ShapeDtypeStruct((third // (n * m), width), BF),
            jax.ShapeDtypeStruct((1, fine_dev), F32),
        ),
        in_specs=[hbm] * 6,
        out_specs=[vmem] * 4,
        scratch_shapes=[
            pltpu.VMEM((n, 1, count), jnp.int32),
            pltpu.VMEM((n, 1, fine_dev), jnp.int32),
            pltpu.VMEM((m, 1, middle), jnp.int32),
            pltpu.VMEM((1, third), jnp.int32),
            pltpu.SMEM((4,), F32),
            pltpu.VMEM((count, width), BF),
            pltpu.VMEM((chunks, n, count // 2, LANES), BF),
            pltpu.VMEM((chunks, total_rows // 2, LANES), BF),
            pltpu.VMEM((total_rows, share), BF),
            pltpu.VMEM((fine, total_rows), BF),
            pltpu.VMEM((middle, total_rows), BF),
            pltpu.VMEM((total_rows, fine), BF),
            pltpu.VMEM((fine, middle), BF),
            pltpu.VMEM((third, m * middle), BF),
            pltpu.VMEM((m * middle, third), BF),
            pltpu.VMEM((chunks, middle, LANES), F32),
            pltpu.VMEM((chunks, fine // 2, LANES), F32),
            pltpu.VMEM((fine // 2, LANES), F32),
            pltpu.VMEM((middle, LANES), F32),
            pltpu.VMEM((fine, LANES), F32),
            pltpu.VMEM((chunks, HALF, middle), BF),
            pltpu.VMEM((chunks, m, HALF // 4, middle), BF),
            pltpu.VMEM((1, middle), F32),
            pltpu.VMEM((m, 1, middle), F32),
            pltpu.VMEM((1, third), F32),
            pltpu.VMEM((1, LANES), F32),
            pltpu.VMEM((chunks, HALF // 4, third), BF),
            pltpu.VMEM((chunks, HALF // 4, m * middle), BF),
            pltpu.VMEM((chunks, HALF, middle), BF),
            pltpu.VMEM((chunks, HALF, window), BF),
            pltpu.VMEM((middle, LANES), F32),
            pltpu.VMEM((chunks, n, fine_dev // 2, LANES), BF),
            pltpu.VMEM((chunks, n, fine_dev // 2, LANES), BF),
            pltpu.VMEM((fine, share), BF),
            pltpu.VMEM((middle, share), BF),
            pltpu.VMEM((window, share), BF),
            pltpu.VMEM((n, 1, fine_dev), F32),
            pltpu.VMEM((n, 1, fine_dev), F32),
            pltpu.VMEM((n, 1, fine_dev), F32),
            dma((6,)),
            dma((2,)),
            dma((2,)),
            dma,
            dma,
            dma,
            dma((chunks,)),
            dma,
            dma((chunks,)),
            dma,
            dma,
            dma((2,)),
            dma((chunks,)),
            dma((tiles,)),
            dma,
            dma((tiles,)),
            dma,
            dma,
            dma,
            dma,
            dma,
            dma,
            dma((2,)),
        ],
        compiler_params=pltpu.CompilerParams(
            collective_id=0, has_side_effects=True, vmem_limit_bytes=40 << 20
        ),
        name="sweep",
    )(
        stay(fine_assign.reshape(1, count)),
        stay(parent1.reshape(1, fine_dev)),
        stay(parent2.reshape(1, middle)),
        stay(parent3.reshape(1, third)),
        stay(shrink),
        stay(rows),
    )
    fine_out, mid_out, coarse_out, spread = settle(fine_out, mid_out, coarse_out, spread)
    return fine_out, mid_out, coarse_out, spread.reshape(fine_dev)


def fits(rows, fine_assign, parent1, parent2, parent3):
    n = lax.axis_size("clus")
    m = lax.axis_size("dp")
    return (
        rows.shape[1] == 2 * n * LANES
        and m % 4 == 0
        and rows.shape[0] % (2 * LANES) == 0
        and parent1.shape[0] % (2 * LANES) == 0
        and parent2.shape[0] % LANES == 0
        and parent2.shape[0] <= 256
        and parent2.shape[0] % (n * 16) == 0
        and parent3.shape[0] % (m // 2 * LANES) == 0
        and parent3.shape[0] // (m // 2) <= parent2.shape[0]
        and parent3.shape[0] % (n * m * 16) == 0
    )


def step(rows, fine_assign, parent1, parent2, parent3, shrink):
    form = fused if fits(rows, fine_assign, parent1, parent2, parent3) else local
    return form(rows, fine_assign, parent1, parent2, parent3, shrink)


def solution(mesh):
    placed = (P(("dp", "clus"), None), P(("dp", "clus")), P(("dp", "clus")), P("dp"), P(), P())
    return jax.shard_map(
        step,
        mesh=mesh,
        in_specs=placed,
        out_specs=(
            P(("dp", "clus"), None),
            P(("dp", "clus"), None),
            P(("dp", "clus"), None),
            P(("dp", "clus")),
        ),
        check_vma=False,
    )
```
